1024 devices in a mesh: ctx: 64 (over z, y), head: 8 (over x), pipe: 2 (over core).
Axes of the slice: x: 8, y: 8, z: 8, core: 2. Of those that a mesh axis runs over, the one named last changes fastest.
Arguments:
- queries: bfloat16 [2, 16384, 4096], P('pipe', 'ctx', 'head'), may hold values from -0.52734375 to 0.52734375
- keys: bfloat16 [2, 16384, 4096], P('pipe', 'ctx', 'head'), may hold values from -0.52734375 to 0.52734375
- values: bfloat16 [2, 16384, 4096], P('pipe', 'ctx', 'head'), may hold values from -0.52734375 to 0.52734375
- out_grad: bfloat16 [2, 16384, 4096], P('pipe', 'ctx', 'head'), may hold values from -6 to 6
- log_decay: float32 [2, 32, 16384], P('pipe', 'head', 'ctx'), may hold values from -1 to 0
- segment_ids: int32 [2, 16384], P('pipe', 'ctx'), may hold values from 0 to 15, never falling along the last dimension, each value on 1 to 2048 neighbouring positions
- w_value: bfloat16 [2, 6144, 4096], P('pipe', None, 'head'), may hold values from -0.09375 to 0.09375
Outputs:
- grad_queries: bfloat16 [2, 16384, 4096], P('pipe', 'ctx', 'head')
- grad_keys: bfloat16 [2, 16384, 4096], P('pipe', 'ctx', 'head')
- grad_values: bfloat16 [2, 16384, 4096], P('pipe', 'ctx', 'head')
- grad_input_prev: bfloat16 [2, 16384, 6144], P('pipe', 'ctx', 'head')
The draws below stay inside these ranges and needn't reach their ends.
Inputs may be any that keep to these rules, and one draw needn't show every extreme that they name: `segment_ids`: never falls along a section's tokens; each document holds at most 2048 tokens, and one holds exactly that many.
All inputs are finite; a program needn't handle non-finite values.
Results may differ from the reference program's by a relative error of at most 0.027.
Values may be sent and summed in bfloat16 or wider, within the bound.
No kernel may reach another device: no remote copies, remote signals or barrier semaphores. Data moves between devices by JAX's collectives and lax.ppermute only.
A program may use at most 64 MiB of HBM per device.

```python
import math
import jax
import jax.numpy as jnp
import numpy as np
from jax import lax

D = 6144
HEADS = 32
DH = 128
TOKENS_PER_SHARD = 256
SECTIONS = 2
TOKENS = 16384
DOC_MAX = 2048
DOCS = 16
N_CTX = 64
N_HEAD = 8


def draw_log_decay(key, part):
    concurrent_lanes = jax.random.split(key, 6)
    head_shape = (SECTIONS, HEADS, 1)
    entire_dimensions = (SECTIONS, HEADS, TOKENS)
    fast_share = 0.5
    picks = jax.random.uniform(concurrent_lanes[0], head_shape, jnp.float32)
    slow_rate = jnp.exp(jax.random.uniform(concurrent_lanes[1], head_shape, jnp.float32, math.log(1e-05), math.log(0.0002)))
    fast_rate = jnp.exp(jax.random.uniform(concurrent_lanes[2], head_shape, jnp.float32, math.log(0.02), math.log(0.035)))
    default_forgetting_speed = jnp.where(picks < fast_share, fast_rate, slow_rate)
    rough_approximation = jnp.exp(jax.random.uniform(concurrent_lanes[3], entire_dimensions, jnp.float32, -math.log(2.0), math.log(2.0)))
    cluster_batches = jax.random.uniform(concurrent_lanes[4], entire_dimensions, jnp.float32) < 1.0 / 1024.0
    network_level_count = jnp.log(jax.random.uniform(concurrent_lanes[5], entire_dimensions, jnp.float32, 0.5, 0.8))
    return -default_forgetting_speed * rough_approximation + jnp.where(cluster_batches, network_level_count, 0.0)


def block_levels(own_key, dims, cuts, least, top_value):
    def one(position, shards_of):
        draws = jax.random.uniform(jax.random.fold_in(jax.random.fold_in(own_key, 6), position), (shards_of,), jnp.float32, least / len(cuts), top_value / len(cuts))
        return jnp.repeat(jnp.exp(draws), dims[position] // shards_of).reshape((-1,) + (1,) * (len(dims) - position - 1))

    level = one(*cuts[0])
    for cut in cuts[1:]:
        level = level * one(*cut)
    return level


def profile(count, total, most, skew):
    loads = [(1 << 20) // math.isqrt(rank ** skew) + 1 for rank in range(2, count + 1)]
    spare, holding = total - most - (count - 1), [1] * (count - 1)
    while spare > 0:
        free = [i for i in range(count - 1) if holding[i] < most]
        pool, budget = sum([loads[i] for i in free]), spare
        for i in free:
            addition = min(most - holding[i], max(1, budget * loads[i] // pool), spare)
            holding[i] = holding[i] + addition
            spare = spare - addition
    return np.array([most] + holding)


def ragged(own_key, count, total, most, slope):
    if count == 2:
        one = jax.random.randint(own_key, (), max(1, total - most), min(most, total - 1) + 1)
        return jnp.stack([one, total - one])
    sizes = jnp.asarray(profile(count, total, most, slope), jnp.int32)
    twos = (count - 1) // 2
    source_of, sink = sizes[1:1 + 2 * twos:2], sizes[2:2 + 2 * twos:2]
    slack = jnp.minimum(source_of - 1, most - sink)
    passed = jax.random.randint(jax.random.fold_in(own_key, 1), (twos,), 0, 1 << 20) % (slack + 1)
    sizes = sizes.at[1:1 + 2 * twos:2].set(source_of - passed).at[2:2 + 2 * twos:2].set(sink + passed)
    return sizes[jax.random.permutation(jax.random.fold_in(own_key, 2), count)]


def bell_draw(rng, dims, spread, bound, cuts=(), dtype=jnp.bfloat16):
    drawn = jax.random.normal(rng, dims, jnp.float32) * spread
    if len(cuts) > 0:
        drawn = block_levels(rng, dims, cuts, -0.22, 0.18) * drawn
    return jnp.clip(drawn, min=-bound, max=bound).astype(dtype)


def setup_inputs(seed: int = 0) -> dict:
    splits = jax.random.split(jax.random.key(seed), 8)
    queries = bell_draw(splits[0], (SECTIONS, TOKENS, HEADS * DH), (DH ** -0.5), 0.52734375, ((0, 2), (1, 64), (2, 8)))
    keys = bell_draw(splits[1], (SECTIONS, TOKENS, HEADS * DH), (DH ** -0.5), 0.52734375, ((0, 2), (1, 64), (2, 8)))
    values = bell_draw(splits[2], (SECTIONS, TOKENS, HEADS * DH), (DH ** -0.5), 0.52734375, ((0, 2), (1, 64), (2, 8)))
    out_grad = bell_draw(splits[3], (SECTIONS, TOKENS, HEADS * DH), 1.0, 6.0, ((0, 2), (1, 64), (2, 8)))
    log_decay = draw_log_decay(jax.random.fold_in(splits[7], 71), 0)
    segment_ids = jax.vmap(lambda own: jnp.searchsorted(jnp.cumsum(ragged(own, DOCS, TOKENS, DOC_MAX, 2)), jnp.arange(TOKENS), side="right"))(jax.random.split(splits[5], SECTIONS)).reshape((SECTIONS, TOKENS)).astype(jnp.int32)
    w_value = bell_draw(splits[6], (SECTIONS, D, HEADS * DH), (HEADS * DH) ** -0.5, 0.09375, ((0, 2), (2, 8)))
    return dict(queries=queries, keys=keys, values=values, out_grad=out_grad, log_decay=log_decay, segment_ids=segment_ids, w_value=w_value)


precise = lax.Precision.HIGHEST


def forward_states(seg_blocks, rate_blocks, key_blocks, value_blocks):
    def advance(carried, block_items):
        state_in, doc_tag = carried
        seg_ids, rates, key_rows, value_rows = block_items
        cumulative = jnp.cumsum(rates, axis=-1)
        decay_end = cumulative[:, -1]
        first_id = seg_ids[0]
        last_id = seg_ids[-1]
        carry_on = jnp.where((first_id == last_id) & (doc_tag == last_id), jnp.float32(1.0), jnp.float32(0.0))
        coefficient_line = jnp.where(seg_ids[None, :] == last_id, jnp.exp(decay_end[:, None] - cumulative), jnp.float32(0.0))
        local_sum = jnp.einsum('thd,ht,the->hde', key_rows.astype(jnp.float32), coefficient_line, value_rows.astype(jnp.float32), precision=precise)
        updated = (carry_on * jnp.exp(decay_end))[:, None, None] * state_in + local_sum
        return (updated, last_id), (state_in, doc_tag)

    initial = (jnp.zeros((HEADS, DH, DH), jnp.float32), jnp.int32(-1))
    _, outputs = lax.scan(advance, initial, (seg_blocks, rate_blocks, key_blocks, value_blocks))
    return outputs


def backward_states(seg_blocks, rate_blocks, query_blocks, grad_blocks):
    def advance(carried, block_items):
        state_in, doc_tag = carried
        seg_ids, rates, query_rows, grad_rows = block_items
        cumulative = jnp.cumsum(rates, axis=-1)
        decay_end = cumulative[:, -1]
        first_id = seg_ids[0]
        last_id = seg_ids[-1]
        carry_on = jnp.where((first_id == last_id) & (doc_tag == last_id), jnp.float32(1.0), jnp.float32(0.0))
        coefficient_line = jnp.where(seg_ids[None, :] == first_id, jnp.exp(cumulative), jnp.float32(0.0))
        local_sum = jnp.einsum('thd,ht,the->hde', query_rows.astype(jnp.float32), coefficient_line, grad_rows.astype(jnp.float32), precision=precise)
        updated = (carry_on * jnp.exp(decay_end))[:, None, None] * state_in + local_sum
        return (updated, first_id), (state_in, doc_tag)

    initial = (jnp.zeros((HEADS, DH, DH), jnp.float32), jnp.int32(-1))
    _, outputs = lax.scan(advance, initial, (seg_blocks, rate_blocks, query_blocks, grad_blocks), reverse=True)
    return outputs


def finalize(block_items):
    seg_ids, rates, query_rows, key_rows, value_rows, grad_rows, fwd_state, fwd_tag, bwd_state, bwd_tag = block_items
    cumulative = jnp.cumsum(rates, axis=-1)
    decay_end = cumulative[:, -1]
    positions = jnp.arange(TOKENS_PER_SHARD)
    causal = (positions[None, :] <= positions[:, None]) & (seg_ids[:, None] == seg_ids[None, :])
    gaps = cumulative[:, :, None] - cumulative[:, None, :]
    decay_weights = jnp.where(causal[None], jnp.exp(jnp.where(causal[None], gaps, jnp.float32(0.0))), jnp.float32(0.0))
    query_f = query_rows.astype(jnp.float32)
    key_f = key_rows.astype(jnp.float32)
    value_f = value_rows.astype(jnp.float32)
    grad_f = grad_rows.astype(jnp.float32)
    value_scores = (jnp.einsum('thd,shd->hts', grad_f, value_f) * decay_weights).astype(jnp.bfloat16).astype(jnp.float32)
    key_scores = (jnp.einsum('thd,shd->hts', query_f, key_f) * decay_weights).astype(jnp.bfloat16).astype(jnp.float32)
    fwd_carry = fwd_state.astype(jnp.bfloat16).astype(jnp.float32)
    bwd_carry = bwd_state.astype(jnp.bfloat16).astype(jnp.float32)
    fwd_gain = jnp.where(seg_ids[None, :] == fwd_tag, jnp.exp(cumulative), jnp.float32(0.0)).T[:, :, None]
    bwd_gain = jnp.where(seg_ids[None, :] == bwd_tag, jnp.exp(decay_end[:, None] - cumulative), jnp.float32(0.0)).T[:, :, None]
    grad_query = jnp.einsum('hts,shd->thd', value_scores, key_f) + fwd_gain * jnp.einsum('the,hde->thd', grad_f, fwd_carry)
    grad_key = jnp.einsum('hts,thd->shd', value_scores, query_f) + bwd_gain * jnp.einsum('the,hde->thd', value_f, bwd_carry)
    grad_value = jnp.einsum('hts,thd->shd', key_scores, grad_f) + bwd_gain * jnp.einsum('thd,hde->the', key_f, bwd_carry)
    return grad_query.astype(jnp.bfloat16), grad_key.astype(jnp.bfloat16), grad_value.astype(jnp.bfloat16)


def input_gradient(grad_value_flat, weight_matrix):
    group_width = HEADS * DH // N_HEAD
    summed = jnp.zeros((TOKENS, D), jnp.float32)
    for group_index in range(N_HEAD):
        lower = group_index * group_width
        term = jnp.dot(grad_value_flat[:, lower:lower + group_width], weight_matrix[:, lower:lower + group_width].T, preferred_element_type=jnp.float32).astype(jnp.bfloat16)
        summed = summed + lax.optimization_barrier(term).astype(jnp.float32)
    return summed.astype(jnp.bfloat16)


def reference(queries, keys, values, out_grad, log_decay, segment_ids, w_value):
    query_out, key_out, value_out, input_out = [], [], [], []
    for section_index in range(SECTIONS):
        def to_blocks(array):
            return array[section_index].reshape(N_CTX, TOKENS_PER_SHARD, HEADS, DH)

        query_blocks = to_blocks(queries)
        key_blocks = to_blocks(keys)
        value_blocks = to_blocks(values)
        grad_blocks = to_blocks(out_grad)
        seg_blocks = segment_ids[section_index].reshape(N_CTX, TOKENS_PER_SHARD)
        rate_blocks = log_decay[section_index].reshape(HEADS, N_CTX, TOKENS_PER_SHARD).transpose(1, 0, 2)
        fwd_state, fwd_tag = forward_states(seg_blocks, rate_blocks, key_blocks, value_blocks)
        bwd_state, bwd_tag = backward_states(seg_blocks, rate_blocks, query_blocks, grad_blocks)
        grad_query, grad_key, grad_value = lax.map(finalize, (seg_blocks, rate_blocks, query_blocks, key_blocks, value_blocks, grad_blocks, fwd_state, fwd_tag, bwd_state, bwd_tag))
        grad_value_flat = grad_value.reshape(TOKENS, HEADS * DH)
        query_out.append(grad_query.reshape(TOKENS, HEADS * DH))
        key_out.append(grad_key.reshape(TOKENS, HEADS * DH))
        value_out.append(grad_value_flat)
        input_out.append(input_gradient(grad_value_flat, w_value[section_index]))
    grad_input = jnp.stack(input_out)
    return jnp.stack(query_out), jnp.stack(key_out), jnp.stack(value_out), jnp.roll(grad_input, -1, axis=0)
```

```python
import jax
import jax.numpy as jnp
import numpy as np
from jax import lax
from jax.experimental import pallas as pl
from jax.experimental.pallas import tpu as pltpu
from jax.sharding import Mesh
from jax.sharding import PartitionSpec as P

f32, bf16 = jnp.float32, jnp.bfloat16
HIGHEST = lax.Precision.HIGHEST
ROW = 8
META = 16
NEVER = -1e30


def dot(a, b, dims):
    return lax.dot_general(a, b, (dims, ((), ())), preferred_element_type=f32)


def iota2(n, axis):
    return lax.broadcasted_iota(jnp.int32, (n, n), axis)


def cumulative_columns(rates):
    n = rates.shape[1]
    lower = (iota2(n, 1) <= iota2(n, 0)).astype(f32)
    return lax.dot_general(lower, rates, (((1,), (1,)), ((), ())), precision=HIGHEST, preferred_element_type=f32)


def cumulative_rows(rates):
    n = rates.shape[1]
    upper = (iota2(n, 0) <= iota2(n, 1)).astype(f32)
    return lax.dot_general(rates, upper, (((1,), (0,)), ((), ())), precision=HIGHEST, preferred_element_type=f32)


def write_message(out, h, state, first, last, through, width):
    share = state.shape[0] // 2
    high = through.astype(bf16)
    low = (through - high.astype(f32)).astype(bf16)
    row = lax.broadcasted_iota(jnp.int32, (META, width), 0)
    meta = jnp.where(row == 0, first, jnp.where(row == 1, last, 0.0))
    meta = jnp.where(row == 2, high.astype(f32), jnp.where(row == 3, low.astype(f32), meta)).astype(bf16)
    for half in range(2):
        p = 2 * h + half
        out[p, 0:share, :] = state[half * share : (half + 1) * share].astype(bf16)
        out[p, share : share + META, :] = meta


def ids_column(seg_row):
    n = seg_row.shape[1]
    on_diagonal = iota2(n, 0) == iota2(n, 1)
    return jnp.sum(jnp.where(on_diagonal, seg_row[...].astype(f32), 0.0), axis=1, keepdims=True)


def block_ids(seg):
    n = seg.shape[0]
    return seg[0:1, :], seg[n - 1 : n, :]


def backward_local_kernel(q, o, rates, seg_row, out):
    cum = cumulative_columns(rates[0])
    heads = rates.shape[1]
    n = cum.shape[0]
    dh = q.shape[2] // heads
    seg = ids_column(seg_row)
    first, last = block_ids(seg)
    scale = jnp.where(seg == seg[0:1, :], jnp.exp(cum), 0.0)
    for h in range(heads):
        cols = slice(h * dh, (h + 1) * dh)
        scaled = (q[0, :, cols].astype(f32) * scale[:, h : h + 1]).astype(bf16)
        state = dot(scaled, o[0, :, cols], ((0,), (0,)))
        write_message(out, h, state, first, last, jnp.exp(cum[n - 1 : n, h : h + 1]), dh)


def scores(a, b, weight):
    return (dot(a, b, ((1,), (1,))) * weight).astype(bf16)


def decay_weight(cum_col, cum_row, keep):
    return jnp.exp(jnp.where(keep, cum_col - cum_row, NEVER))


def forward_local_kernel(q, k, v, o, rates, seg_row, out, gv, gain):
    cum = cumulative_columns(rates[0])
    cum_t = cumulative_rows(rates[0])
    heads = rates.shape[1]
    n = cum.shape[0]
    dh = q.shape[2] // heads
    seg = ids_column(seg_row)
    first, last = block_ids(seg)
    keep = (iota2(n, 1) <= iota2(n, 0)) & (seg == seg_row[...].astype(f32))
    scale = jnp.where(seg == seg[n - 1 : n, :], jnp.exp(cum[n - 1 : n, :] - cum), 0.0)
    for h in range(heads):
        cols = slice(h * dh, (h + 1) * dh)
        kh = k[0, :, cols]
        scaled = (kh.astype(f32) * scale[:, h : h + 1]).astype(bf16)
        state = dot(scaled, v[0, :, cols], ((0,), (0,)))
        write_message(out, h, state, first, last, jnp.exp(cum[n - 1 : n, h : h + 1]), dh)
        weight = decay_weight(cum[:, h : h + 1], cum_t[h : h + 1, :], keep)
        ks = scores(q[0, :, cols], kh, weight)
        gv[:, cols] = dot(ks, o[0, :, cols], ((0,), (0,)))
        gain[:, h * dh : (h + 1) * dh] = jnp.broadcast_to(scale[:, h : h + 1], (n, dh))


def unpack(msg, y):
    share = msg.shape[1] - META
    block = msg[y].astype(f32)
    meta = block[share:, :]
    return block[:share], meta[0:1], meta[1:2], meta[2:3] + meta[3:4]


def order(reverse):
    return range(ROW - 1, -1, -1) if reverse else range(ROW)


def row_total_kernel(reverse, msg, out):
    share = msg.shape[1] - META
    tag, total = None, None
    for y in order(reverse):
        state, first, last, through = unpack(msg, y)
        if total is None:
            total = state
        else:
            same = jnp.where((first == last) & (tag == last), through, 0.0)
            total = same * total + state
        tag = first if reverse else last
    out[0:share, :] = total.astype(bf16)
    out[share:, :] = jnp.broadcast_to(tag, (META, tag.shape[1])).astype(bf16)


def row_scan_kernel(reverse, msg, carried, out):
    share = msg.shape[1] - META
    running = carried[0:share, :].astype(f32)
    tag = carried[share : share + META, :].astype(f32)[0:1]
    for y in order(reverse):
        state, first, last, through = unpack(msg, y)
        edge = last if reverse else first
        out[y] = jnp.where(edge == tag, running, 0.0).astype(bf16)
        same = jnp.where((first == last) & (tag == last), through, 0.0)
        running = same * running + state
        tag = first if reverse else last


def weight_kernel(local, gain, k, state, w, gv, out, kept):
    heads = gv.shape[1] // state.shape[1]
    dh = state.shape[1]

    @pl.when(pl.program_id(0) == 0)
    def _():
        for h in range(heads):
            cols = slice(h * dh, (h + 1) * dh)
            b = state[h * dh : (h + 1) * dh, :]
            far = dot(k[0, :, cols], b, ((1,), (0,)))
            kept[:, cols] = (local[:, cols] + gain[:, cols] * far).astype(bf16)
        gv[...] = kept[...]

    out[0] = dot(kept[...], w[0], ((1,), (1,))).astype(bf16)


def query_key_kernel(q, k, v, o, rates, seg_row, fwd, bwd, gain, dq, dk):
    cum = cumulative_columns(rates[0])
    cum_t = cumulative_rows(rates[0])
    heads = rates.shape[1]
    n = cum.shape[0]
    dh = q.shape[2] // heads
    seg = ids_column(seg_row)
    keep = (iota2(n, 1) <= iota2(n, 0)) & (seg == seg_row[...].astype(f32))
    reach = jnp.where(seg == seg[0:1, :], jnp.exp(cum), 0.0)
    for h in range(heads):
        cols = slice(h * dh, (h + 1) * dh)
        weight = decay_weight(cum[:, h : h + 1], cum_t[h : h + 1, :], keep)
        vs = scores(o[0, :, cols], v[0, :, cols], weight)
        f = fwd[h * dh : (h + 1) * dh, :]
        b = bwd[h * dh : (h + 1) * dh, :]
        far_q = dot(o[0, :, cols], f, ((1,), (1,)))
        far_k = dot(v[0, :, cols], b, ((1,), (1,)))
        dq[:, cols] = (dot(vs, k[0, :, cols], ((1,), (0,))) + reach[:, h : h + 1] * far_q).astype(bf16)
        dk[:, cols] = (dot(vs, q[0, :, cols], ((0,), (0,))) + gain[:, cols] * far_k).astype(bf16)


def call(kernel, shapes, name):
    return pl.pallas_call(kernel, out_shape=shapes, name=name)


def body(queries, keys, values, out_grad, log_decay, segment_ids, w_value):
    n, width = queries.shape[1:]
    heads = log_decay.shape[1]
    dh = width // heads
    rows = lax.axis_size("plane")
    groups = lax.axis_size("head")
    share = heads * dh // ROW
    message = jax.ShapeDtypeStruct((ROW, share + META, dh), bf16)
    total = jax.ShapeDtypeStruct((share + META, dh), bf16)
    states = jax.ShapeDtypeStruct((ROW, share, dh), bf16)

    def exchange(array):
        return lax.all_to_all(array, "line", 0, 0, tiled=True)

    def relay(msg, reverse, tag):
        own = call(lambda *refs: row_total_kernel(reverse, *refs), total, "total_" + tag)(msg)
        pairs = [(z, z - 1) for z in range(1, rows)] if reverse else [(z - 1, z) for z in range(1, rows)]
        return lax.ppermute(own, "plane", pairs)

    def scan(msg, carried, reverse, tag):
        out = call(lambda *refs: row_scan_kernel(reverse, *refs), states, "scan_" + tag)(msg, carried)
        return exchange(out).reshape(heads * dh, dh)

    sent = call(backward_local_kernel, message, "backward_local")(queries, out_grad, log_decay, segment_ids)
    got = exchange(sent)
    carried = relay(got, True, "backward")
    fwd_sent, gv_local, gain = call(
        forward_local_kernel,
        (message, jax.ShapeDtypeStruct((n, width), f32), jax.ShapeDtypeStruct((n, width), f32)),
        "forward_local",
    )(queries, keys, values, out_grad, log_decay, segment_ids)
    bwd = scan(got, carried, True, "backward")

    slice_rows = w_value.shape[1] // groups
    whole = lambda *shape: pl.BlockSpec(shape, lambda i: (0,) * len(shape))
    grad_value, partials = pl.pallas_call(
        weight_kernel,
        grid=(groups,),
        in_specs=[
            whole(n, width),
            whole(n, width),
            whole(1, n, width),
            whole(heads * dh, dh),
            pl.BlockSpec((1, slice_rows, width), lambda i: (i, 0, 0)),
        ],
        out_specs=[whole(n, width), pl.BlockSpec((1, n, slice_rows), lambda i: (i, 0, 0))],
        out_shape=(
            jax.ShapeDtypeStruct((n, width), bf16),
            jax.ShapeDtypeStruct((groups, n, slice_rows), bf16),
        ),
        scratch_shapes=[pltpu.VMEM((n, width), bf16)],
        name="weight",
    )(gv_local, gain, keys, bwd, w_value.reshape(groups, slice_rows, width))
    fwd_sent, partials = lax.optimization_barrier((fwd_sent, partials))
    summed = lax.psum_scatter(partials, "head", scatter_dimension=0, tiled=False)

    fwd_got = exchange(fwd_sent)
    fwd = scan(fwd_got, relay(fwd_got, False, "forward"), False, "forward")
    summed, fwd = lax.optimization_barrier((summed, fwd))
    grad_query, grad_key = call(
        query_key_kernel,
        (jax.ShapeDtypeStruct((n, width), bf16), jax.ShapeDtypeStruct((n, width), bf16)),
        "query_key",
    )(queries, keys, values, out_grad, log_decay, segment_ids, fwd, bwd, gain)

    sections = lax.axis_size("pipe")
    shifted = lax.ppermute(summed, "pipe", [((i + 1) % sections, i) for i in range(sections)])
    return (grad_query[None], grad_key[None], grad_value[None], shifted[None])


def solution(mesh):
    ctx, head, pipe = (mesh.shape[name] for name in ("ctx", "head", "pipe"))
    grid = Mesh(np.asarray(mesh.devices).reshape(ctx // ROW, ROW, head, pipe), ("plane", "line", "head", "pipe"))
    seq = ("plane", "line")
    tokens = P("pipe", seq, "head")
    return jax.shard_map(
        body,
        mesh=grid,
        in_specs=(tokens, tokens, tokens, tokens, P("pipe", "head", seq), P("pipe", seq), P("pipe", None, "head")),
        out_specs=(tokens, tokens, tokens, tokens),
        check_vma=False,
    )
```

```python
import jax
import jax.numpy as jnp
import numpy as np
from jax import lax
from jax.experimental import pallas as pl
from jax.experimental.pallas import tpu as pltpu
from jax.sharding import Mesh
from jax.sharding import PartitionSpec as P

f32, bf16 = jnp.float32, jnp.bfloat16
HIGHEST = lax.Precision.HIGHEST
ROW = 8
META = 16
NEVER = -1e30


def dot(a, b, dims):
    return lax.dot_general(a, b, (dims, ((), ())), preferred_element_type=f32)


def iota2(n, axis):
    return lax.broadcasted_iota(jnp.int32, (n, n), axis)


def cumulative_columns(rates):
    n = rates.shape[1]
    lower = (iota2(n, 1) <= iota2(n, 0)).astype(f32)
    return lax.dot_general(lower, rates, (((1,), (1,)), ((), ())), precision=HIGHEST, preferred_element_type=f32)


def cumulative_rows(rates):
    n = rates.shape[1]
    upper = (iota2(n, 0) <= iota2(n, 1)).astype(f32)
    return lax.dot_general(rates, upper, (((1,), (0,)), ((), ())), precision=HIGHEST, preferred_element_type=f32)


def write_message(out, h, state, first, last, through, width):
    share = state.shape[0] // 2
    high = through.astype(bf16)
    low = (through - high.astype(f32)).astype(bf16)
    row = lax.broadcasted_iota(jnp.int32, (META, width), 0)
    meta = jnp.where(row == 0, first, jnp.where(row == 1, last, 0.0))
    meta = jnp.where(row == 2, high.astype(f32), jnp.where(row == 3, low.astype(f32), meta)).astype(bf16)
    for half in range(2):
        p = 2 * h + half
        out[p, 0:share, :] = state[half * share : (half + 1) * share].astype(bf16)
        out[p, share : share + META, :] = meta


def ids_column(seg_row):
    n = seg_row.shape[1]
    on_diagonal = iota2(n, 0) == iota2(n, 1)
    return jnp.sum(jnp.where(on_diagonal, seg_row[...].astype(f32), 0.0), axis=1, keepdims=True)


def block_ids(seg):
    n = seg.shape[0]
    return seg[0:1, :], seg[n - 1 : n, :]


def fetch(sources, targets, sems):
    copies = [pltpu.make_async_copy(src, dst, sems.at[i]) for i, (src, dst) in enumerate(zip(sources, targets))]
    for copy in copies:
        copy.start()
    return copies


def backward_local_kernel(rates_in, seg_in, q_in, o_in, out, rates, seg_row, q, o, sems):
    rates_copy, seg_copy, q_copy, o_copy = fetch((rates_in, seg_in, q_in, o_in), (rates, seg_row, q, o), sems)
    rates_copy.wait()
    cum = cumulative_columns(rates[0])
    heads = rates.shape[1]
    n = cum.shape[0]
    dh = q.shape[2] // heads
    seg_copy.wait()
    seg = ids_column(seg_row)
    first, last = block_ids(seg)
    scale = jnp.where(seg == seg[0:1, :], jnp.exp(cum), 0.0)
    q_copy.wait()
    o_copy.wait()
    for h in range(heads):
        cols = slice(h * dh, (h + 1) * dh)
        scaled = (q[0, :, cols].astype(f32) * scale[:, h : h + 1]).astype(bf16)
        state = dot(scaled, o[0, :, cols], ((0,), (0,)))
        write_message(out, h, state, first, last, jnp.exp(cum[n - 1 : n, h : h + 1]), dh)


def scores(a, b, weight):
    return (dot(a, b, ((1,), (1,))) * weight).astype(bf16)


def decay_weight(cum_col, cum_row, keep):
    return jnp.exp(jnp.where(keep, cum_col - cum_row, NEVER))


def forward_local_kernel(
    rates_in, seg_in, k_in, v_in, q_in, o_in, out, gv, gain, k, rates, seg_row, v, q, o, sems
):
    sources = (rates_in, seg_in, k_in, v_in, q_in, o_in)
    rates_copy, seg_copy, *others = fetch(sources, (rates, seg_row, k, v, q, o), sems)
    rates_copy.wait()
    cum = cumulative_columns(rates[0])
    cum_t = cumulative_rows(rates[0])
    heads = rates.shape[1]
    n = cum.shape[0]
    dh = q.shape[2] // heads
    seg_copy.wait()
    seg = ids_column(seg_row)
    first, last = block_ids(seg)
    keep = (iota2(n, 1) <= iota2(n, 0)) & (seg == seg_row[...].astype(f32))
    scale = jnp.where(seg == seg[n - 1 : n, :], jnp.exp(cum[n - 1 : n, :] - cum), 0.0)
    for copy in others:
        copy.wait()
    for h in range(heads):
        cols = slice(h * dh, (h + 1) * dh)
        kh = k[0, :, cols]
        scaled = (kh.astype(f32) * scale[:, h : h + 1]).astype(bf16)
        state = dot(scaled, v[0, :, cols], ((0,), (0,)))
        write_message(out, h, state, first, last, jnp.exp(cum[n - 1 : n, h : h + 1]), dh)
        weight = decay_weight(cum[:, h : h + 1], cum_t[h : h + 1, :], keep)
        ks = scores(q[0, :, cols], kh, weight)
        gv[:, cols] = dot(ks, o[0, :, cols], ((0,), (0,)))
        gain[:, cols] = jnp.broadcast_to(scale[:, h : h + 1], (n, dh))


def unpack(msg, y):
    share = msg.shape[1] - META
    block = msg[y].astype(f32)
    meta = block[share:, :]
    return block[:share], meta[0:1], meta[1:2], meta[2:3] + meta[3:4]


def order(reverse):
    return range(ROW - 1, -1, -1) if reverse else range(ROW)


def row_total_kernel(reverse, msg, out):
    share = msg.shape[1] - META
    tag, total = None, None
    for y in order(reverse):
        state, first, last, through = unpack(msg, y)
        if total is None:
            total = state
        else:
            same = jnp.where((first == last) & (tag == last), through, 0.0)
            total = same * total + state
        tag = first if reverse else last
    out[0:share, :] = total.astype(bf16)
    out[share:, :] = jnp.broadcast_to(tag, (META, tag.shape[1])).astype(bf16)


def row_scan_kernel(reverse, msg, carried, out):
    share = msg.shape[1] - META
    running = carried[0:share, :].astype(f32)
    tag = carried[share : share + META, :].astype(f32)[0:1]
    for y in order(reverse):
        state, first, last, through = unpack(msg, y)
        edge = last if reverse else first
        out[y] = jnp.where(edge == tag, running, 0.0).astype(bf16)
        same = jnp.where((first == last) & (tag == last), through, 0.0)
        running = same * running + state
        tag = first if reverse else last


LOADS = 4


def weight_kernel(local, gain, k, state, w_in, gv, out, kept, w, made, in_sems, out_sems):
    pieces = w.shape[0]
    loads = fetch([w_in.at[0, i] for i in range(pieces)], [w.at[i] for i in range(pieces)], in_sems)
    heads = gv.shape[1] // state.shape[1]
    dh = state.shape[1]
    for h in range(heads):
        cols = slice(h * dh, (h + 1) * dh)
        b = state[h * dh : (h + 1) * dh, :]
        far = dot(k[0, :, cols], b, ((1,), (0,)))
        kept[:, cols] = (local[:, cols] + gain[:, cols] * far).astype(bf16)
    gv[...] = kept[...]
    step = out.shape[2]
    each = out.shape[0] // pieces
    copies = []
    for i in range(pieces):
        loads[i].wait()
        for j in range(each):
            rows = w[i, j * step : (j + 1) * step, :]
            made[i * each + j] = dot(kept[...], rows, ((1,), (1,))).astype(bf16)
        span = pl.ds(i * each, each)
        copy = pltpu.make_async_copy(made.at[span], out.at[span], out_sems.at[i])
        copy.start()
        copies.append(copy)
    for copy in copies:
        copy.wait()


def query_key_kernel(
    rates_in, seg_in, q_in, k_in, v_in, o_in, fwd, bwd, gain, dq, dk, rates, seg_row, q, k, v, o, sems
):
    sources = (rates_in, seg_in, q_in, k_in, v_in, o_in)
    for copy in fetch(sources, (rates, seg_row, q, k, v, o), sems):
        copy.wait()
    cum = cumulative_columns(rates[0])
    cum_t = cumulative_rows(rates[0])
    heads = rates.shape[1]
    n = cum.shape[0]
    dh = q.shape[2] // heads
    seg = ids_column(seg_row)
    keep = (iota2(n, 1) <= iota2(n, 0)) & (seg == seg_row[...].astype(f32))
    reach = jnp.where(seg == seg[0:1, :], jnp.exp(cum), 0.0)
    for h in range(heads):
        cols = slice(h * dh, (h + 1) * dh)
        weight = decay_weight(cum[:, h : h + 1], cum_t[h : h + 1, :], keep)
        vs = scores(o[0, :, cols], v[0, :, cols], weight)
        f = fwd[h * dh : (h + 1) * dh, :]
        b = bwd[h * dh : (h + 1) * dh, :]
        far_q = dot(o[0, :, cols], f, ((1,), (1,)))
        far_k = dot(v[0, :, cols], b, ((1,), (1,)))
        dq[:, cols] = (dot(vs, k[0, :, cols], ((1,), (0,))) + reach[:, h : h + 1] * far_q).astype(bf16)
        dk[:, cols] = (dot(vs, q[0, :, cols], ((0,), (0,))) + gain[:, cols] * far_k).astype(bf16)


IN_VMEM = pl.BlockSpec(memory_space=pltpu.VMEM)
IN_HBM = pl.BlockSpec(memory_space=pltpu.HBM)


def call(kernel, shapes, name, mib=4, in_specs=None, out_specs=IN_VMEM, scratch=()):
    def run(*args):
        specs = in_specs or [IN_VMEM] * len(args)
        args = [pltpu.with_memory_space_constraint(a, pltpu.HBM) if spec is IN_HBM else a for a, spec in zip(args, specs)]
        return pl.pallas_call(
            kernel,
            in_specs=specs,
            out_specs=jax.tree.map(lambda _: IN_VMEM, shapes) if out_specs is IN_VMEM else out_specs,
            out_shape=shapes,
            scratch_shapes=scratch,
            compiler_params=pltpu.CompilerParams(vmem_limit_bytes=mib << 20),
            name=name,
        )(*args)

    return run


def body(queries, keys, values, out_grad, log_decay, segment_ids, w_value):
    n, width = queries.shape[1:]
    heads = log_decay.shape[1]
    dh = width // heads
    rows = lax.axis_size("plane")
    groups = lax.axis_size("head")
    share = heads * dh // ROW
    message = jax.ShapeDtypeStruct((ROW, share + META, dh), bf16)
    total = jax.ShapeDtypeStruct((share + META, dh), bf16)
    states = pltpu.VMEM((ROW, share, dh), bf16)

    def exchange(array):
        return lax.all_to_all(array, "line", 0, 0, tiled=True)

    def relay(msg, reverse, tag):
        own = call(lambda *refs: row_total_kernel(reverse, *refs), total, "total_" + tag)(msg)
        pairs = [(z, z - 1) for z in range(1, rows)] if reverse else [(z - 1, z) for z in range(1, rows)]
        return lax.ppermute(own, "plane", pairs)

    def scan(msg, carried, reverse, tag):
        out = call(lambda *refs: row_scan_kernel(reverse, *refs), states, "scan_" + tag)(msg, carried)
        return exchange(out).reshape(heads * dh, dh)

    block = pltpu.VMEM((1, n, width), bf16)
    small = [pltpu.VMEM(log_decay.shape, f32), pltpu.VMEM(segment_ids.shape, jnp.int32)]
    sent = call(
        backward_local_kernel,
        message,
        "backward_local",
        mib=12,
        in_specs=[IN_HBM] * 4,
        scratch=[*small, block, block, pltpu.SemaphoreType.DMA((4,))],
    )(log_decay, segment_ids, queries, out_grad)
    got = exchange(sent)
    carried = relay(got, True, "backward")
    fwd_sent, gv_local, gain, keys_near = call(
        forward_local_kernel,
        (
            message,
            pltpu.VMEM((n, width), f32),
            pltpu.VMEM((n, width), f32),
            block,
        ),
        "forward_local",
        mib=12,
        in_specs=[IN_HBM] * 6,
        scratch=[*small, block, block, block, pltpu.SemaphoreType.DMA((6,))],
    )(log_decay, segment_ids, keys, values, queries, out_grad)
    bwd = scan(got, carried, True, "backward")

    step = w_value.shape[1] // groups
    pieces = LOADS if groups % LOADS == 0 else 1
    piece_rows = w_value.shape[1] // pieces
    grad_value, partials = call(
        weight_kernel,
        (
            jax.ShapeDtypeStruct((n, width), bf16),
            jax.ShapeDtypeStruct((groups, n, step), bf16),
        ),
        "weight",
        mib=18,
        in_specs=[IN_VMEM] * 4 + [IN_HBM],
        out_specs=(IN_VMEM, IN_HBM),
        scratch=[
            pltpu.VMEM((n, width), bf16),
            pltpu.VMEM((pieces, piece_rows, width), bf16),
            pltpu.VMEM((groups, n, step), bf16),
            pltpu.SemaphoreType.DMA((pieces,)),
            pltpu.SemaphoreType.DMA((pieces,)),
        ],
    )(gv_local, gain, keys_near, bwd, w_value.reshape(1, pieces, piece_rows, width))
    fwd_sent, partials = lax.optimization_barrier((fwd_sent, partials))
    summed = lax.psum_scatter(partials, "head", scatter_dimension=0, tiled=False)

    fwd_got = exchange(fwd_sent)
    fwd = scan(fwd_got, relay(fwd_got, False, "forward"), False, "forward")
    grad_query, grad_key = call(
        query_key_kernel,
        (jax.ShapeDtypeStruct((n, width), bf16), jax.ShapeDtypeStruct((n, width), bf16)),
        "query_key",
        mib=12,
        in_specs=[IN_HBM] * 6 + [IN_VMEM] * 3,
        scratch=[*small, block, block, block, block, pltpu.SemaphoreType.DMA((6,))],
    )(log_decay, segment_ids, queries, keys, values, out_grad, fwd, bwd, gain)

    summed, grad_query, grad_key = lax.optimization_barrier((summed, grad_query, grad_key))
    sections = lax.axis_size("pipe")
    shifted = lax.ppermute(summed, "pipe", [((i + 1) % sections, i) for i in range(sections)])
    return (grad_query[None], grad_key[None], grad_value[None], shifted[None])


def solution(mesh):
    ctx, head, pipe = (mesh.shape[name] for name in ("ctx", "head", "pipe"))
    grid = Mesh(np.asarray(mesh.devices).reshape(ctx // ROW, ROW, head, pipe), ("plane", "line", "head", "pipe"))
    seq = ("plane", "line")
    tokens = P("pipe", seq, "head")
    return jax.shard_map(
        body,
        mesh=grid,
        in_specs=(tokens, tokens, tokens, tokens, P("pipe", "head", seq), P("pipe", seq), P("pipe", None, "head")),
        out_specs=(tokens, tokens, tokens, tokens),
        check_vma=False,
    )
```

```python
import jax
import jax.numpy as jnp
import numpy as np
from jax import lax
from jax.experimental import pallas as pl
from jax.experimental.pallas import tpu as pltpu
from jax.sharding import Mesh
from jax.sharding import PartitionSpec as P

f32, bf16 = jnp.float32, jnp.bfloat16
HIGHEST = lax.Precision.HIGHEST
ROW = 8
META = 16
NEVER = -1e30


def dot(a, b, dims):
    return lax.dot_general(a, b, (dims, ((), ())), preferred_element_type=f32)


def iota2(n, axis):
    return lax.broadcasted_iota(jnp.int32, (n, n), axis)


def cumulative_columns(rates):
    n = rates.shape[1]
    lower = (iota2(n, 1) <= iota2(n, 0)).astype(f32)
    return lax.dot_general(lower, rates, (((1,), (1,)), ((), ())), precision=HIGHEST, preferred_element_type=f32)


def cumulative_rows(rates):
    n = rates.shape[1]
    upper = (iota2(n, 0) <= iota2(n, 1)).astype(f32)
    return lax.dot_general(rates, upper, (((1,), (0,)), ((), ())), precision=HIGHEST, preferred_element_type=f32)


def write_message(out, h, states, first, last, through, width):
    share = states[0].shape[0] // 2
    high = through.astype(bf16)
    low = (through - high.astype(f32)).astype(bf16)
    row = lax.broadcasted_iota(jnp.int32, (META, width), 0)
    meta = jnp.where(row == 0, first, jnp.where(row == 1, last, 0.0))
    meta = jnp.where(row == 2, high.astype(f32), jnp.where(row == 3, low.astype(f32), meta)).astype(bf16)
    for half in range(2):
        p = 2 * h + half
        for i, state in enumerate(states):
            out[p, i * share : (i + 1) * share, :] = state[half * share : (half + 1) * share].astype(bf16)
        out[p, 2 * share : 2 * share + META, :] = meta


def ids_column(seg_row):
    n = seg_row.shape[1]
    on_diagonal = iota2(n, 0) == iota2(n, 1)
    return jnp.sum(jnp.where(on_diagonal, seg_row[...].astype(f32), 0.0), axis=1, keepdims=True)


def block_ids(seg):
    n = seg.shape[0]
    return seg[0:1, :], seg[n - 1 : n, :]


def fetch(sources, targets, sems):
    copies = [pltpu.make_async_copy(src, dst, sems.at[i]) for i, (src, dst) in enumerate(zip(sources, targets))]
    for copy in copies:
        copy.start()
    return copies


def local_kernel(rates_in, seg_in, q_in, o_in, k_in, v_in, out, rates, seg_row, q, o, k, v, sems):
    sources = (rates_in, seg_in, q_in, o_in, k_in, v_in)
    rates_copy, seg_copy, *others = fetch(sources, (rates, seg_row, q, o, k, v), sems)
    rates_copy.wait()
    cum = cumulative_columns(rates[0])
    heads = rates.shape[1]
    n = cum.shape[0]
    dh = q.shape[2] // heads
    seg_copy.wait()
    seg = ids_column(seg_row)
    first, last = block_ids(seg)
    ahead = jnp.where(seg == seg[0:1, :], jnp.exp(cum), 0.0)
    behind = jnp.where(seg == seg[n - 1 : n, :], jnp.exp(cum[n - 1 : n, :] - cum), 0.0)
    for copy in others:
        copy.wait()
    for h in range(heads):
        cols = slice(h * dh, (h + 1) * dh)
        scaled_q = (q[0, :, cols].astype(f32) * ahead[:, h : h + 1]).astype(bf16)
        scaled_k = (k[0, :, cols].astype(f32) * behind[:, h : h + 1]).astype(bf16)
        states = (dot(scaled_q, o[0, :, cols], ((0,), (0,))), dot(scaled_k, v[0, :, cols], ((0,), (0,))))
        write_message(out, h, states, first, last, jnp.exp(cum[n - 1 : n, h : h + 1]), dh)


def scores(a, b, weight):
    return (dot(a, b, ((1,), (1,))) * weight).astype(bf16)


def decay_weight(cum_col, cum_row, keep):
    return jnp.exp(jnp.where(keep, cum_col - cum_row, NEVER))


def near_kernel(rates_in, seg_in, k_in, q_in, o_in, gv, gain, k, rates, seg_row, q, o, sems):
    sources = (rates_in, seg_in, k_in, q_in, o_in)
    rates_copy, seg_copy, *others = fetch(sources, (rates, seg_row, k, q, o), sems)
    rates_copy.wait()
    cum = cumulative_columns(rates[0])
    cum_t = cumulative_rows(rates[0])
    heads = rates.shape[1]
    n = cum.shape[0]
    dh = q.shape[2] // heads
    seg_copy.wait()
    seg = ids_column(seg_row)
    keep = (iota2(n, 1) <= iota2(n, 0)) & (seg == seg_row[...].astype(f32))
    behind = jnp.where(seg == seg[n - 1 : n, :], jnp.exp(cum[n - 1 : n, :] - cum), 0.0)
    for copy in others:
        copy.wait()
    for h in range(heads):
        cols = slice(h * dh, (h + 1) * dh)
        weight = decay_weight(cum[:, h : h + 1], cum_t[h : h + 1, :], keep)
        ks = scores(q[0, :, cols], k[0, :, cols], weight)
        gv[:, cols] = dot(ks, o[0, :, cols], ((0,), (0,)))
        gain[:, cols] = jnp.broadcast_to(behind[:, h : h + 1], (n, dh))


def unpack(msg, y, reverse):
    share = (msg.shape[1] - META) // 2
    start = 0 if reverse else share
    meta = msg[y, 2 * share : 2 * share + META, :].astype(f32)
    state = msg[y, start : start + share, :].astype(f32)
    return state, meta[0:1], meta[1:2], meta[2:3] + meta[3:4]


def order(reverse):
    return range(ROW - 1, -1, -1) if reverse else range(ROW)


def row_total_kernel(msg, out_backward, out_forward):
    for out, reverse in ((out_backward, True), (out_forward, False)):
        share = out.shape[0] - META
        tag, total = None, None
        for y in order(reverse):
            state, first, last, through = unpack(msg, y, reverse)
            if total is None:
                total = state
            else:
                same = jnp.where((first == last) & (tag == last), through, 0.0)
                total = same * total + state
            tag = first if reverse else last
        out[0:share, :] = total.astype(bf16)
        out[share:, :] = jnp.broadcast_to(tag, (META, tag.shape[1])).astype(bf16)


def row_scan_kernel(msg, carried_backward, carried_forward, out):
    for carried, reverse in ((carried_backward, True), (carried_forward, False)):
        share = carried.shape[0] - META
        start = 0 if reverse else share
        running = carried[0:share, :].astype(f32)
        tag = carried[share : share + META, :].astype(f32)[0:1]
        for y in order(reverse):
            state, first, last, through = unpack(msg, y, reverse)
            edge = last if reverse else first
            out[y, start : start + share, :] = jnp.where(edge == tag, running, 0.0).astype(bf16)
            same = jnp.where((first == last) & (tag == last), through, 0.0)
            running = same * running + state
            tag = first if reverse else last


def head_state(states, h, reverse):
    share = states.shape[1] // 2
    start = 0 if reverse else share
    return jnp.concatenate([states[2 * h + half, start : start + share, :] for half in range(2)], axis=0)


def far_kernel(me, local, gain, k, states, w_in, gv, low, high, w, sem):
    groups = w_in.shape[0]
    copy = pltpu.make_async_copy(w_in.at[lax.rem(me[0] + groups // 2, groups)], w, sem)
    copy.start()
    dh = states.shape[2]
    for h in range(gv.shape[1] // dh):
        cols = slice(h * dh, (h + 1) * dh)
        far = dot(k[0, :, cols], head_state(states, h, True), ((1,), (0,)))
        gv[:, cols] = (local[:, cols] + gain[:, cols] * far).astype(bf16)
    copy.wait()
    rows = low.shape[0]
    low[...] = dot(gv[0:rows, :], w[...], ((1,), (1,))).astype(bf16)
    high[...] = dot(gv[rows:, :], w[...], ((1,), (1,))).astype(bf16)


def offsets(groups):
    return [sign * far for far in range(groups // 2 - 1, 0, -1) for sign in (-1, 1)] + [0]


def partial_kernel(me, gv, w_in, out, w, sems):
    groups = w_in.shape[0]
    wanted = offsets(groups)
    sources = [w_in.at[lax.rem(me[0] + groups + offset, groups)] for offset in wanted]
    copies = fetch(sources, [w.at[i] for i in range(len(wanted))], sems)
    for i, copy in enumerate(copies):
        copy.wait()
        out[i] = dot(gv[...], w[i], ((1,), (1,))).astype(bf16)


def add_kernel(index, partials, *refs):
    *arrived, out = refs
    total = partials[index].astype(f32)
    for first, ref in arrived:
        rows = ref.shape[0]
        if rows == total.shape[0]:
            total = total + ref[...].astype(f32)
        else:
            kept = [total[0:first], total[first : first + rows] + ref[...].astype(f32), total[first + rows :]]
            total = jnp.concatenate([part for part in kept if part.shape[0]], axis=0)
    out[...] = total.astype(bf16)


def query_key_kernel(
    rates_in, seg_in, q_in, k_in, v_in, o_in, states, gain, dq, dk, rates, seg_row, q, k, v, o, sems
):
    sources = (rates_in, seg_in, q_in, k_in, v_in, o_in)
    for copy in fetch(sources, (rates, seg_row, q, k, v, o), sems):
        copy.wait()
    cum = cumulative_columns(rates[0])
    cum_t = cumulative_rows(rates[0])
    heads = rates.shape[1]
    n = cum.shape[0]
    dh = q.shape[2] // heads
    seg = ids_column(seg_row)
    keep = (iota2(n, 1) <= iota2(n, 0)) & (seg == seg_row[...].astype(f32))
    reach = jnp.where(seg == seg[0:1, :], jnp.exp(cum), 0.0)
    for h in range(heads):
        cols = slice(h * dh, (h + 1) * dh)
        weight = decay_weight(cum[:, h : h + 1], cum_t[h : h + 1, :], keep)
        vs = scores(o[0, :, cols], v[0, :, cols], weight)
        f = head_state(states, h, False)
        b = head_state(states, h, True)
        far_q = dot(o[0, :, cols], f, ((1,), (1,)))
        far_k = dot(v[0, :, cols], b, ((1,), (1,)))
        dq[:, cols] = (dot(vs, k[0, :, cols], ((1,), (0,))) + reach[:, h : h + 1] * far_q).astype(bf16)
        dk[:, cols] = (dot(vs, q[0, :, cols], ((0,), (0,))) + gain[:, cols] * far_k).astype(bf16)


IN_VMEM = pl.BlockSpec(memory_space=pltpu.VMEM)
IN_SMEM = pl.BlockSpec(memory_space=pltpu.SMEM)
IN_HBM = pl.BlockSpec(memory_space=pltpu.HBM)


def call(kernel, shapes, name, mib=4, in_specs=None, out_specs=IN_VMEM, scratch=()):
    def run(*args):
        specs = in_specs or [IN_VMEM] * len(args)
        args = [pltpu.with_memory_space_constraint(a, pltpu.HBM) if spec is IN_HBM else a for a, spec in zip(args, specs)]
        return pl.pallas_call(
            kernel,
            in_specs=specs,
            out_specs=jax.tree.map(lambda _: IN_VMEM, shapes) if out_specs is IN_VMEM else out_specs,
            out_shape=shapes,
            scratch_shapes=scratch,
            compiler_params=pltpu.CompilerParams(vmem_limit_bytes=mib << 20),
            name=name,
        )(*args)

    return run


def body(queries, keys, values, out_grad, log_decay, segment_ids, w_value):
    n, width = queries.shape[1:]
    heads = log_decay.shape[1]
    dh = width // heads
    planes = lax.axis_size("plane")
    groups = lax.axis_size("head")
    share = heads * dh // ROW
    step = w_value.shape[1] // groups
    half = groups // 2
    block = pltpu.VMEM((1, n, width), bf16)
    small = [pltpu.VMEM(log_decay.shape, f32), pltpu.VMEM(segment_ids.shape, jnp.int32)]
    dma = pltpu.SemaphoreType.DMA

    def exchange(array):
        return lax.all_to_all(array, "line", 0, 0, tiled=True)

    sent = call(
        local_kernel,
        pltpu.VMEM((ROW, 2 * share + META, dh), bf16),
        "local",
        mib=12,
        in_specs=[IN_HBM] * 6,
        scratch=[*small, block, block, block, block, dma((6,))],
    )(log_decay, segment_ids, queries, out_grad, keys, values)
    got = exchange(sent)
    total = pltpu.VMEM((share + META, dh), bf16)
    total_backward, total_forward = call(row_total_kernel, (total, total), "row_total")(got)
    up = [(z - 1, z) for z in range(1, planes)]
    down = [(z, z - 1) for z in range(1, planes)]
    carried_backward = lax.ppermute(total_backward, "plane", down)
    carried_forward = lax.ppermute(total_forward, "plane", up)
    scanned = call(row_scan_kernel, pltpu.VMEM((ROW, 2 * share, dh), bf16), "row_scan")(
        got, carried_backward, carried_forward
    )
    states = exchange(scanned)
    gv_local, gain, keys_near = call(
        near_kernel,
        (pltpu.VMEM((n, width), f32), pltpu.VMEM((n, width), f32), block),
        "near",
        mib=12,
        in_specs=[IN_HBM] * 5,
        scratch=[*small, block, block, dma((5,))],
    )(log_decay, segment_ids, keys, queries, out_grad)

    me = lax.axis_index("head").astype(jnp.int32).reshape(1)
    weights = w_value.reshape(groups, step, width)
    piece = pltpu.VMEM((n // 2, step), bf16)
    grad_value, low, high = call(
        far_kernel,
        (pltpu.VMEM((n, width), bf16), piece, piece),
        "far",
        mib=12,
        in_specs=[IN_SMEM] + [IN_VMEM] * 4 + [IN_HBM],
        scratch=[pltpu.VMEM((step, width), bf16), dma],
    )(me, gv_local, gain, keys_near, states, weights)
    partials = call(
        partial_kernel,
        pltpu.VMEM((groups - 1, n, step), bf16),
        "partial",
        mib=16,
        in_specs=[IN_SMEM, IN_VMEM, IN_HBM],
        scratch=[pltpu.VMEM((groups - 1, step, width), bf16), dma((groups - 1,))],
    )(me, grad_value, weights)
    grad_query, grad_key = call(
        query_key_kernel,
        (jax.ShapeDtypeStruct((n, width), bf16), jax.ShapeDtypeStruct((n, width), bf16)),
        "query_key",
        mib=12,
        in_specs=[IN_HBM] * 6 + [IN_VMEM] * 2,
        scratch=[*small, block, block, block, block, dma((6,))],
    )(log_decay, segment_ids, queries, keys, values, out_grad, states, gain)

    before = [(i, (i - 1) % groups) for i in range(groups)]
    after = [(i, (i + 1) % groups) for i in range(groups)]
    firsts = (0, n // 2)

    def add(index, arrived, starts, name):
        def kernel(partials_ref, *refs):
            add_kernel(index, partials_ref, *zip(starts, refs[:-1]), refs[-1])

        return call(kernel, pltpu.VMEM((n, step), bf16), name)(partials, *arrived)

    for i in range(half):
        low = lax.ppermute(low, "head", before)
        high = lax.ppermute(high, "head", after)
        starts = firsts if i == 0 else (0, 0)
        if i == half - 1:
            summed = add(groups - 2, (low, high), starts, "add_last")
        else:
            low = add(2 * i, (low,), starts[:1], "add_low")
            high = add(2 * i + 1, (high,), starts[1:], "add_high")
        if i == 1:
            low, high, grad_query, grad_key = lax.optimization_barrier((low, high, grad_query, grad_key))

    sections = lax.axis_size("pipe")
    shifted = lax.ppermute(summed, "pipe", [((i + 1) % sections, i) for i in range(sections)])
    return (grad_query[None], grad_key[None], grad_value[None], shifted[None])


def solution(mesh):
    ctx, head, pipe = (mesh.shape[name] for name in ("ctx", "head", "pipe"))
    grid = Mesh(np.asarray(mesh.devices).reshape(ctx // ROW, ROW, head, pipe), ("plane", "line", "head", "pipe"))
    seq = ("plane", "line")
    tokens = P("pipe", seq, "head")
    return jax.shard_map(
        body,
        mesh=grid,
        in_specs=(tokens, tokens, tokens, tokens, P("pipe", "head", seq), P("pipe", seq), P("pipe", None, "head")),
        out_specs=(tokens, tokens, tokens, tokens),
        check_vma=False,
    )
```

```python
import jax
import jax.numpy as jnp
import numpy as np
from jax import lax
from jax.experimental import pallas as pl
from jax.experimental.pallas import tpu as pltpu
from jax.sharding import Mesh
from jax.sharding import PartitionSpec as P

f32, bf16 = jnp.float32, jnp.bfloat16
HIGHEST = lax.Precision.HIGHEST
ROW = 8
META = 16
NEVER = -1e30


def dot(a, b, dims):
    return lax.dot_general(a, b, (dims, ((), ())), preferred_element_type=f32)


def iota2(n, axis):
    return lax.broadcasted_iota(jnp.int32, (n, n), axis)


def cumulative_columns(rates):
    n = rates.shape[1]
    lower = (iota2(n, 1) <= iota2(n, 0)).astype(f32)
    return lax.dot_general(lower, rates, (((1,), (1,)), ((), ())), precision=HIGHEST, preferred_element_type=f32)


def cumulative_rows(rates):
    n = rates.shape[1]
    upper = (iota2(n, 0) <= iota2(n, 1)).astype(f32)
    return lax.dot_general(rates, upper, (((1,), (0,)), ((), ())), precision=HIGHEST, preferred_element_type=f32)


def write_message(out, h, states, first, last, through, width):
    share = states[0].shape[0] // 2
    high = through.astype(bf16)
    low = (through - high.astype(f32)).astype(bf16)
    row = lax.broadcasted_iota(jnp.int32, (META, width), 0)
    meta = jnp.where(row == 0, first, jnp.where(row == 1, last, 0.0))
    meta = jnp.where(row == 2, high.astype(f32), jnp.where(row == 3, low.astype(f32), meta)).astype(bf16)
    for half in range(2):
        p = 2 * h + half
        for i, state in enumerate(states):
            out[p, i * share : (i + 1) * share, :] = state[half * share : (half + 1) * share].astype(bf16)
        out[p, 2 * share : 2 * share + META, :] = meta


def ids_column(seg_row):
    n = seg_row.shape[1]
    on_diagonal = iota2(n, 0) == iota2(n, 1)
    return jnp.sum(jnp.where(on_diagonal, seg_row[...].astype(f32), 0.0), axis=1, keepdims=True)


def block_ids(seg):
    n = seg.shape[0]
    return seg[0:1, :], seg[n - 1 : n, :]


def fetch(sources, targets, sems):
    copies = [pltpu.make_async_copy(src, dst, sems.at[i]) for i, (src, dst) in enumerate(zip(sources, targets))]
    for copy in copies:
        copy.start()
    return copies


def local_kernel(rates_in, seg_in, q_in, o_in, k_in, v_in, out, rates, seg_row, q, o, k, v, sems):
    sources = (rates_in, seg_in, q_in, o_in, k_in, v_in)
    rates_copy, seg_copy, *others = fetch(sources, (rates, seg_row, q, o, k, v), sems)
    rates_copy.wait()
    cum = cumulative_columns(rates[0])
    heads = rates.shape[1]
    n = cum.shape[0]
    dh = q.shape[2] // heads
    seg_copy.wait()
    seg = ids_column(seg_row)
    first, last = block_ids(seg)
    ahead = jnp.where(seg == seg[0:1, :], jnp.exp(cum), 0.0)
    behind = jnp.where(seg == seg[n - 1 : n, :], jnp.exp(cum[n - 1 : n, :] - cum), 0.0)
    for copy in others:
        copy.wait()
    for h in range(heads):
        cols = slice(h * dh, (h + 1) * dh)
        scaled_q = (q[0, :, cols].astype(f32) * ahead[:, h : h + 1]).astype(bf16)
        scaled_k = (k[0, :, cols].astype(f32) * behind[:, h : h + 1]).astype(bf16)
        states = (dot(scaled_q, o[0, :, cols], ((0,), (0,))), dot(scaled_k, v[0, :, cols], ((0,), (0,))))
        write_message(out, h, states, first, last, jnp.exp(cum[n - 1 : n, h : h + 1]), dh)


def scores(a, b, weight):
    return (dot(a, b, ((1,), (1,))) * weight).astype(bf16)


def decay_weight(cum_col, cum_row, keep):
    return jnp.exp(jnp.where(keep, cum_col - cum_row, NEVER))


def near_kernel(place, rates_in, seg_in, k_in, q_in, o_in, w_in, gv, gain, k, w, rates, seg_row, q, o, sems):
    groups = w_in.shape[0]
    w_far = w_in.at[destination(place, groups // 2, groups)]
    sources = (rates_in, seg_in, k_in, q_in, o_in, w_far)
    rates_copy, seg_copy, *others, w_copy = fetch(sources, (rates, seg_row, k, q, o, w), sems)
    rates_copy.wait()
    cum = cumulative_columns(rates[0])
    cum_t = cumulative_rows(rates[0])
    heads = rates.shape[1]
    n = cum.shape[0]
    dh = q.shape[2] // heads
    seg_copy.wait()
    seg = ids_column(seg_row)
    keep = (iota2(n, 1) <= iota2(n, 0)) & (seg == seg_row[...].astype(f32))
    behind = jnp.where(seg == seg[n - 1 : n, :], jnp.exp(cum[n - 1 : n, :] - cum), 0.0)
    for copy in others:
        copy.wait()
    for h in range(heads):
        cols = slice(h * dh, (h + 1) * dh)
        weight = decay_weight(cum[:, h : h + 1], cum_t[h : h + 1, :], keep)
        ks = scores(q[0, :, cols], k[0, :, cols], weight)
        gv[:, cols] = dot(ks, o[0, :, cols], ((0,), (0,)))
        gain[:, cols] = jnp.broadcast_to(behind[:, h : h + 1], (n, dh))
    w_copy.wait()


def unpack(msg, y, reverse):
    share = (msg.shape[1] - META) // 2
    start = 0 if reverse else share
    meta = msg[y, 2 * share : 2 * share + META, :].astype(f32)
    state = msg[y, start : start + share, :].astype(f32)
    return state, meta[0:1], meta[1:2], meta[2:3] + meta[3:4]


def order(reverse):
    return range(ROW - 1, -1, -1) if reverse else range(ROW)


def row_total_kernel(msg, out_backward, out_forward):
    for out, reverse in ((out_backward, True), (out_forward, False)):
        share = out.shape[0] - META
        tag, total = None, None
        for y in order(reverse):
            state, first, last, through = unpack(msg, y, reverse)
            if total is None:
                total = state
            else:
                same = jnp.where((first == last) & (tag == last), through, 0.0)
                total = same * total + state
            tag = first if reverse else last
        out[0:share, :] = total.astype(bf16)
        out[share:, :] = jnp.broadcast_to(tag, (META, tag.shape[1])).astype(bf16)


def row_scan_kernel(msg, carried_backward, carried_forward, out):
    for carried, reverse in ((carried_backward, True), (carried_forward, False)):
        share = carried.shape[0] - META
        start = 0 if reverse else share
        running = carried[0:share, :].astype(f32)
        tag = carried[share : share + META, :].astype(f32)[0:1]
        for y in order(reverse):
            state, first, last, through = unpack(msg, y, reverse)
            edge = last if reverse else first
            out[y, start : start + share, :] = jnp.where(edge == tag, running, 0.0).astype(bf16)
            same = jnp.where((first == last) & (tag == last), through, 0.0)
            running = same * running + state
            tag = first if reverse else last


def head_state(states, h, reverse):
    share = states.shape[1] // 2
    start = 0 if reverse else share
    return jnp.concatenate([states[2 * h + half, start : start + share, :] for half in range(2)], axis=0)


def destination(place, offset, groups):
    return lax.rem(place[0] + groups + place[1] * offset, groups)


def far_kernel(place, local, gain, k, states, w, gv, low, high):
    dh = states.shape[2]
    for h in range(gv.shape[1] // dh):
        cols = slice(h * dh, (h + 1) * dh)
        far = dot(k[0, :, cols], head_state(states, h, True), ((1,), (0,)))
        gv[:, cols] = (local[:, cols] + gain[:, cols] * far).astype(bf16)
    rows = low.shape[0]
    low[...] = dot(gv[0:rows, :], w[...], ((1,), (1,))).astype(bf16)
    high[...] = dot(gv[rows:, :], w[...], ((1,), (1,))).astype(bf16)


def offsets(groups):
    return [sign * far for far in range(groups // 2 - 1, 0, -1) for sign in (-1, 1)] + [0]


def partial_kernel(wanted, place, gv, w_in, out, *rest):
    *gv_out, w, sems = rest
    groups = w_in.shape[0]
    sources = [w_in.at[destination(place, offset, groups)] for offset in wanted]
    copies = fetch(sources, [w.at[i] for i in range(len(wanted))], sems)
    for target in gv_out:
        copies.append(pltpu.make_async_copy(gv, target, sems.at[len(wanted)]))
        copies[-1].start()
    for i in range(len(wanted)):
        copies[i].wait()
        out[i] = dot(gv[...], w[i], ((1,), (1,))).astype(bf16)
    for copy in copies[len(wanted) :]:
        copy.wait()


def add_kernel(index, partials, *refs):
    *arrived, out = refs
    total = partials[index].astype(f32)
    for first, ref in arrived:
        rows = ref.shape[0]
        if rows == total.shape[0]:
            total = total + ref[...].astype(f32)
        else:
            kept = [total[0:first], total[first : first + rows] + ref[...].astype(f32), total[first + rows :]]
            total = jnp.concatenate([part for part in kept if part.shape[0]], axis=0)
    out[...] = total.astype(bf16)


def query_key_kernel(
    rates_in, seg_in, q_in, k_in, v_in, o_in, states, gain, dq, dk, rates, seg_row, q, k, v, o, sems
):
    sources = (rates_in, seg_in, q_in, k_in, v_in, o_in)
    for copy in fetch(sources, (rates, seg_row, q, k, v, o), sems):
        copy.wait()
    cum = cumulative_columns(rates[0])
    cum_t = cumulative_rows(rates[0])
    heads = rates.shape[1]
    n = cum.shape[0]
    dh = q.shape[2] // heads
    seg = ids_column(seg_row)
    keep = (iota2(n, 1) <= iota2(n, 0)) & (seg == seg_row[...].astype(f32))
    reach = jnp.where(seg == seg[0:1, :], jnp.exp(cum), 0.0)
    for h in range(heads):
        cols = slice(h * dh, (h + 1) * dh)
        weight = decay_weight(cum[:, h : h + 1], cum_t[h : h + 1, :], keep)
        vs = scores(o[0, :, cols], v[0, :, cols], weight)
        f = head_state(states, h, False)
        b = head_state(states, h, True)
        far_q = dot(o[0, :, cols], f, ((1,), (1,)))
        far_k = dot(v[0, :, cols], b, ((1,), (1,)))
        dq[:, cols] = (dot(vs, k[0, :, cols], ((1,), (0,))) + reach[:, h : h + 1] * far_q).astype(bf16)
        dk[:, cols] = (dot(vs, q[0, :, cols], ((0,), (0,))) + gain[:, cols] * far_k).astype(bf16)


IN_VMEM = pl.BlockSpec(memory_space=pltpu.VMEM)
IN_SMEM = pl.BlockSpec(memory_space=pltpu.SMEM)
IN_HBM = pl.BlockSpec(memory_space=pltpu.HBM)


def call(kernel, shapes, name, mib=4, in_specs=None, out_specs=IN_VMEM, scratch=()):
    def run(*args):
        specs = in_specs or [IN_VMEM] * len(args)
        args = [pltpu.with_memory_space_constraint(a, pltpu.HBM) if spec is IN_HBM else a for a, spec in zip(args, specs)]
        return pl.pallas_call(
            kernel,
            in_specs=specs,
            out_specs=jax.tree.map(lambda _: IN_VMEM, shapes) if out_specs is IN_VMEM else out_specs,
            out_shape=shapes,
            scratch_shapes=scratch,
            compiler_params=pltpu.CompilerParams(vmem_limit_bytes=mib << 20),
            name=name,
        )(*args)

    return run


def body(queries, keys, values, out_grad, log_decay, segment_ids, w_value):
    n, width = queries.shape[1:]
    heads = log_decay.shape[1]
    dh = width // heads
    planes = lax.axis_size("plane")
    groups = lax.axis_size("head")
    share = heads * dh // ROW
    step = w_value.shape[1] // groups
    half = groups // 2
    block = pltpu.VMEM((1, n, width), bf16)
    small = [pltpu.VMEM(log_decay.shape, f32), pltpu.VMEM(segment_ids.shape, jnp.int32)]
    dma = pltpu.SemaphoreType.DMA

    def exchange(array):
        return lax.all_to_all(array, "line", 0, 0, tiled=True)

    sent = call(
        local_kernel,
        pltpu.VMEM((ROW, 2 * share + META, dh), bf16),
        "local",
        mib=12,
        in_specs=[IN_HBM] * 6,
        scratch=[*small, block, block, block, block, dma((6,))],
    )(log_decay, segment_ids, queries, out_grad, keys, values)
    got = exchange(sent)
    total = pltpu.VMEM((share + META, dh), bf16)
    total_backward, total_forward = call(row_total_kernel, (total, total), "row_total")(got)
    up = [(z - 1, z) for z in range(1, planes)]
    down = [(z, z - 1) for z in range(1, planes)]
    carried_backward = lax.ppermute(total_backward, "plane", down)
    carried_forward = lax.ppermute(total_forward, "plane", up)
    scanned = call(row_scan_kernel, pltpu.VMEM((ROW, 2 * share, dh), bf16), "row_scan")(
        got, carried_backward, carried_forward
    )
    states = exchange(scanned)
    place = jnp.stack([lax.axis_index("head"), 1 - 2 * (lax.axis_index("pipe") & 1)]).astype(jnp.int32)
    weights = w_value.reshape(groups, step, width)
    gv_local, gain, keys_near, w_far = call(
        near_kernel,
        (pltpu.VMEM((n, width), f32), pltpu.VMEM((n, width), f32), block, pltpu.VMEM((step, width), bf16)),
        "near",
        mib=12,
        in_specs=[IN_SMEM] + [IN_HBM] * 6,
        scratch=[*small, block, block, dma((6,))],
    )(place, log_decay, segment_ids, keys, queries, out_grad, weights)

    piece = pltpu.VMEM((n // 2, step), bf16)
    near_gv, low, high = call(
        far_kernel,
        (pltpu.VMEM((n, width), bf16), piece, piece),
        "far",
        in_specs=[IN_SMEM] + [IN_VMEM] * 5,
    )(place, gv_local, gain, keys_near, states, w_far)
    def products(wanted, gv, name, writes):
        count = len(wanted)
        extra = (jax.ShapeDtypeStruct((n, width), bf16),) if writes else ()
        return call(
            lambda *refs: partial_kernel(wanted, *refs),
            (pltpu.VMEM((count, n, step), bf16), *extra),
            name,
            mib=4 * count,
            in_specs=[IN_SMEM, IN_VMEM, IN_HBM],
            out_specs=(IN_VMEM, *(IN_HBM for _ in extra)),
            scratch=[pltpu.VMEM((count, step, width), bf16), dma((count + 1,))],
        )(place, gv, weights)

    wanted = offsets(groups)
    (soon,) = products(wanted[:2], near_gv, "partial_soon", False)
    grad_query, grad_key = call(
        query_key_kernel,
        (jax.ShapeDtypeStruct((n, width), bf16), jax.ShapeDtypeStruct((n, width), bf16)),
        "query_key",
        mib=12,
        in_specs=[IN_HBM] * 6 + [IN_VMEM] * 2,
        scratch=[*small, block, block, block, block, dma((6,))],
    )(log_decay, segment_ids, queries, keys, values, out_grad, states, gain)

    sections = lax.axis_size("pipe")

    def ring(direction):
        pairs = []
        for i in range(groups):
            for c in range(sections):
                to = (i + (direction if c % 2 == 0 else -direction)) % groups
                pairs.append((i * sections + c, to * sections + c))
        return lambda array: lax.ppermute(array, ("head", "pipe"), pairs)

    before, after = ring(-1), ring(1)
    firsts = (0, n // 2)

    def add(index, arrived, starts, name):
        source, index = (soon, index) if index < 2 else (later, index - 2)

        def kernel(partials_ref, *refs):
            add_kernel(index, partials_ref, *zip(starts, refs[:-1]), refs[-1])

        return call(kernel, pltpu.VMEM((n, step), bf16), name)(source, *arrived)

    for i in range(half):
        low = before(low)
        high = after(high)
        starts = firsts if i == 0 else (0, 0)
        if i == half - 1:
            summed = add(groups - 2, (low, high), starts, "add_last")
        else:
            low = add(2 * i, (low,), starts[:1], "add_low")
            high = add(2 * i + 1, (high,), starts[1:], "add_high")
        if i == 0:
            near_gv, low, high = lax.optimization_barrier((near_gv, low, high))
            later, grad_value = products(wanted[2:], near_gv, "partial_later", True)
        if i == min(2, half - 1):
            low, high, grad_query, grad_key = lax.optimization_barrier((low, high, grad_query, grad_key))

    shifted = lax.ppermute(summed, "pipe", [((i + 1) % sections, i) for i in range(sections)])
    return (grad_query[None], grad_key[None], grad_value[None], shifted[None])


def solution(mesh):
    ctx, head, pipe = (mesh.shape[name] for name in ("ctx", "head", "pipe"))
    grid = Mesh(np.asarray(mesh.devices).reshape(ctx // ROW, ROW, head, pipe), ("plane", "line", "head", "pipe"))
    seq = ("plane", "line")
    tokens = P("pipe", seq, "head")
    return jax.shard_map(
        body,
        mesh=grid,
        in_specs=(tokens, tokens, tokens, tokens, P("pipe", "head", seq), P("pipe", seq), P("pipe", None, "head")),
        out_specs=(tokens, tokens, tokens, tokens),
        check_vma=False,
    )
```

```python
import jax
import jax.numpy as jnp
import numpy as np
from jax import lax
from jax.experimental import pallas as pl
from jax.experimental.pallas import tpu as pltpu
from jax.sharding import Mesh
from jax.sharding import PartitionSpec as P

f32, bf16 = jnp.float32, jnp.bfloat16
HIGHEST = lax.Precision.HIGHEST
ROW = 8
META = 16
NEVER = -1e30


def dot(a, b, dims):
    return lax.dot_general(a, b, (dims, ((), ())), preferred_element_type=f32)


def iota2(n, axis):
    return lax.broadcasted_iota(jnp.int32, (n, n), axis)


def cumulative_columns(rates):
    n = rates.shape[1]
    lower = (iota2(n, 1) <= iota2(n, 0)).astype(f32)
    return lax.dot_general(lower, rates, (((1,), (1,)), ((), ())), precision=HIGHEST, preferred_element_type=f32)


def cumulative_rows(rates):
    n = rates.shape[1]
    upper = (iota2(n, 0) <= iota2(n, 1)).astype(f32)
    return lax.dot_general(rates, upper, (((1,), (0,)), ((), ())), precision=HIGHEST, preferred_element_type=f32)


def write_message(out, h, states, first, last, through, width):
    share = states[0].shape[0] // 2
    high = through.astype(bf16)
    low = (through - high.astype(f32)).astype(bf16)
    row = lax.broadcasted_iota(jnp.int32, (META, width), 0)
    meta = jnp.where(row == 0, first, jnp.where(row == 1, last, 0.0))
    meta = jnp.where(row == 2, high.astype(f32), jnp.where(row == 3, low.astype(f32), meta)).astype(bf16)
    for half in range(2):
        p = 2 * h + half
        for i, state in enumerate(states):
            out[p, i * share : (i + 1) * share, :] = state[half * share : (half + 1) * share].astype(bf16)
        out[p, 2 * share : 2 * share + META, :] = meta


def ids_column(seg_row):
    n = seg_row.shape[1]
    on_diagonal = iota2(n, 0) == iota2(n, 1)
    return jnp.sum(jnp.where(on_diagonal, seg_row[...].astype(f32), 0.0), axis=1, keepdims=True)


def block_ids(seg):
    n = seg.shape[0]
    return seg[0:1, :], seg[n - 1 : n, :]


def fetch(sources, targets, sems):
    copies = [pltpu.make_async_copy(src, dst, sems.at[i]) for i, (src, dst) in enumerate(zip(sources, targets))]
    for copy in copies:
        copy.start()
    return copies


def local_kernel(rates_in, seg_in, q_in, o_in, k_in, v_in, out, rates, seg_row, q, o, k, v, sems):
    sources = (rates_in, seg_in, q_in, o_in, k_in, v_in)
    rates_copy, seg_copy, *others = fetch(sources, (rates, seg_row, q, o, k, v), sems)
    rates_copy.wait()
    cum = cumulative_columns(rates[0])
    heads = rates.shape[1]
    n = cum.shape[0]
    dh = q.shape[2] // heads
    seg_copy.wait()
    seg = ids_column(seg_row)
    first, last = block_ids(seg)
    ahead = jnp.where(seg == seg[0:1, :], jnp.exp(cum), 0.0)
    behind = jnp.where(seg == seg[n - 1 : n, :], jnp.exp(cum[n - 1 : n, :] - cum), 0.0)
    for copy in others:
        copy.wait()
    for h in range(heads):
        cols = slice(h * dh, (h + 1) * dh)
        scaled_q = (q[0, :, cols].astype(f32) * ahead[:, h : h + 1]).astype(bf16)
        scaled_k = (k[0, :, cols].astype(f32) * behind[:, h : h + 1]).astype(bf16)
        states = (dot(scaled_q, o[0, :, cols], ((0,), (0,))), dot(scaled_k, v[0, :, cols], ((0,), (0,))))
        write_message(out, h, states, first, last, jnp.exp(cum[n - 1 : n, h : h + 1]), dh)


def scores(a, b, weight):
    return (dot(a, b, ((1,), (1,))) * weight).astype(bf16)


def decay_weight(cum_col, cum_row, keep):
    return jnp.exp(jnp.where(keep, cum_col - cum_row, NEVER))


def near_kernel(place, rates_in, seg_in, k_in, q_in, o_in, w_in, gv, gain, k, w, rates, seg_row, q, o, sems):
    groups = w_in.shape[0]
    w_far = w_in.at[destination(place, FIRST[0], groups)]
    sources = (rates_in, seg_in, k_in, q_in, o_in, w_far)
    rates_copy, seg_copy, *others, w_copy = fetch(sources, (rates, seg_row, k, q, o, w), sems)
    rates_copy.wait()
    cum = cumulative_columns(rates[0])
    cum_t = cumulative_rows(rates[0])
    heads = rates.shape[1]
    n = cum.shape[0]
    dh = q.shape[2] // heads
    seg_copy.wait()
    seg = ids_column(seg_row)
    keep = (iota2(n, 1) <= iota2(n, 0)) & (seg == seg_row[...].astype(f32))
    behind = jnp.where(seg == seg[n - 1 : n, :], jnp.exp(cum[n - 1 : n, :] - cum), 0.0)
    for copy in others:
        copy.wait()
    for h in range(heads):
        cols = slice(h * dh, (h + 1) * dh)
        weight = decay_weight(cum[:, h : h + 1], cum_t[h : h + 1, :], keep)
        ks = scores(q[0, :, cols], k[0, :, cols], weight)
        gv[:, cols] = dot(ks, o[0, :, cols], ((0,), (0,)))
        gain[:, cols] = jnp.broadcast_to(behind[:, h : h + 1], (n, dh))
    w_copy.wait()


def unpack(msg, y, reverse):
    share = (msg.shape[1] - META) // 2
    start = 0 if reverse else share
    meta = msg[y, 2 * share : 2 * share + META, :].astype(f32)
    state = msg[y, start : start + share, :].astype(f32)
    return state, meta[0:1], meta[1:2], meta[2:3] + meta[3:4]


def order(reverse):
    return range(ROW - 1, -1, -1) if reverse else range(ROW)


def row_total_kernel(msg, out_backward, out_forward):
    for out, reverse in ((out_backward, True), (out_forward, False)):
        share = out.shape[0] - META
        tag, total = None, None
        for y in order(reverse):
            state, first, last, through = unpack(msg, y, reverse)
            if total is None:
                total = state
            else:
                same = jnp.where((first == last) & (tag == last), through, 0.0)
                total = same * total + state
            tag = first if reverse else last
        out[0:share, :] = total.astype(bf16)
        out[share:, :] = jnp.broadcast_to(tag, (META, tag.shape[1])).astype(bf16)


def row_scan_kernel(msg, carried_backward, carried_forward, out):
    for carried, reverse in ((carried_backward, True), (carried_forward, False)):
        share = carried.shape[0] - META
        start = 0 if reverse else share
        running = carried[0:share, :].astype(f32)
        tag = carried[share : share + META, :].astype(f32)[0:1]
        for y in order(reverse):
            state, first, last, through = unpack(msg, y, reverse)
            edge = last if reverse else first
            out[y, start : start + share, :] = jnp.where(edge == tag, running, 0.0).astype(bf16)
            same = jnp.where((first == last) & (tag == last), through, 0.0)
            running = same * running + state
            tag = first if reverse else last


def head_state(states, h, reverse):
    share = states.shape[1] // 2
    start = 0 if reverse else share
    return jnp.concatenate([states[2 * h + half, start : start + share, :] for half in range(2)], axis=0)


def destination(place, offset, groups):
    return lax.rem(place[0] + groups + place[1] * offset, groups)


FIRST = (-4, -2, 3)
SOON = (-3, 2)
LATER = (-1, 1, 0)


def far_kernel(place, local, gain, k, states, w_first, w_in, gv, pair, single, w, sems):
    groups = w_in.shape[0]
    sources = [w_in.at[destination(place, offset, groups)] for offset in FIRST[1:]]
    copies = fetch(sources, [w.at[i] for i in range(len(sources))], sems)
    dh = states.shape[2]
    for h in range(gv.shape[1] // dh):
        cols = slice(h * dh, (h + 1) * dh)
        far = dot(k[0, :, cols], head_state(states, h, True), ((1,), (0,)))
        gv[:, cols] = (local[:, cols] + gain[:, cols] * far).astype(bf16)
    pair[0] = dot(gv[...], w_first[...], ((1,), (1,))).astype(bf16)
    copies[0].wait()
    pair[1] = dot(gv[...], w[0], ((1,), (1,))).astype(bf16)
    copies[1].wait()
    single[...] = dot(gv[...], w[1], ((1,), (1,))).astype(bf16)


def partial_kernel(wanted, place, gv, w_in, out, *rest):
    *gv_out, w, sems = rest
    groups = w_in.shape[0]
    sources = [w_in.at[destination(place, offset, groups)] for offset in wanted]
    copies = fetch(sources, [w.at[i] for i in range(len(wanted))], sems)
    for target in gv_out:
        copies.append(pltpu.make_async_copy(gv, target, sems.at[len(wanted)]))
        copies[-1].start()
    for i in range(len(wanted)):
        copies[i].wait()
        out[i] = dot(gv[...], w[i], ((1,), (1,))).astype(bf16)
    for copy in copies[len(wanted) :]:
        copy.wait()


def add_kernel(own, picks, *refs):
    partials, *arrived, out = refs
    total = partials[own].astype(f32)
    for ref, pick in zip(arrived, picks):
        total = total + (ref[...] if pick is None else ref[pick]).astype(f32)
    out[...] = total.astype(bf16)


def query_key_kernel(
    rates_in, seg_in, q_in, k_in, v_in, o_in, states, gain, dq, dk, rates, seg_row, q, k, v, o, sems
):
    sources = (rates_in, seg_in, q_in, k_in, v_in, o_in)
    for copy in fetch(sources, (rates, seg_row, q, k, v, o), sems):
        copy.wait()
    cum = cumulative_columns(rates[0])
    cum_t = cumulative_rows(rates[0])
    heads = rates.shape[1]
    n = cum.shape[0]
    dh = q.shape[2] // heads
    seg = ids_column(seg_row)
    keep = (iota2(n, 1) <= iota2(n, 0)) & (seg == seg_row[...].astype(f32))
    reach = jnp.where(seg == seg[0:1, :], jnp.exp(cum), 0.0)
    for h in range(heads):
        cols = slice(h * dh, (h + 1) * dh)
        weight = decay_weight(cum[:, h : h + 1], cum_t[h : h + 1, :], keep)
        vs = scores(o[0, :, cols], v[0, :, cols], weight)
        f = head_state(states, h, False)
        b = head_state(states, h, True)
        far_q = dot(o[0, :, cols], f, ((1,), (1,)))
        far_k = dot(v[0, :, cols], b, ((1,), (1,)))
        dq[:, cols] = (dot(vs, k[0, :, cols], ((1,), (0,))) + reach[:, h : h + 1] * far_q).astype(bf16)
        dk[:, cols] = (dot(vs, q[0, :, cols], ((0,), (0,))) + gain[:, cols] * far_k).astype(bf16)


IN_VMEM = pl.BlockSpec(memory_space=pltpu.VMEM)
IN_SMEM = pl.BlockSpec(memory_space=pltpu.SMEM)
IN_HBM = pl.BlockSpec(memory_space=pltpu.HBM)


def call(kernel, shapes, name, mib=4, in_specs=None, out_specs=IN_VMEM, scratch=()):
    def run(*args):
        specs = in_specs or [IN_VMEM] * len(args)
        args = [pltpu.with_memory_space_constraint(a, pltpu.HBM) if spec is IN_HBM else a for a, spec in zip(args, specs)]
        return pl.pallas_call(
            kernel,
            in_specs=specs,
            out_specs=jax.tree.map(lambda _: IN_VMEM, shapes) if out_specs is IN_VMEM else out_specs,
            out_shape=shapes,
            scratch_shapes=scratch,
            compiler_params=pltpu.CompilerParams(vmem_limit_bytes=mib << 20),
            name=name,
        )(*args)

    return run


def body(queries, keys, values, out_grad, log_decay, segment_ids, w_value):
    n, width = queries.shape[1:]
    heads = log_decay.shape[1]
    dh = width // heads
    planes = lax.axis_size("plane")
    groups = lax.axis_size("head")
    share = heads * dh // ROW
    step = w_value.shape[1] // groups
    half = groups // 2
    block = pltpu.VMEM((1, n, width), bf16)
    small = [pltpu.VMEM(log_decay.shape, f32), pltpu.VMEM(segment_ids.shape, jnp.int32)]
    dma = pltpu.SemaphoreType.DMA

    def exchange(array):
        return lax.all_to_all(array, "line", 0, 0, tiled=True)

    sent = call(
        local_kernel,
        pltpu.VMEM((ROW, 2 * share + META, dh), bf16),
        "local",
        mib=12,
        in_specs=[IN_HBM] * 6,
        scratch=[*small, block, block, block, block, dma((6,))],
    )(log_decay, segment_ids, queries, out_grad, keys, values)
    got = exchange(sent)
    total = pltpu.VMEM((share + META, dh), bf16)
    total_backward, total_forward = call(row_total_kernel, (total, total), "row_total")(got)
    up = [(z - 1, z) for z in range(1, planes)]
    down = [(z, z - 1) for z in range(1, planes)]
    carried_backward = lax.ppermute(total_backward, "plane", down)
    carried_forward = lax.ppermute(total_forward, "plane", up)
    scanned = call(row_scan_kernel, pltpu.VMEM((ROW, 2 * share, dh), bf16), "row_scan")(
        got, carried_backward, carried_forward
    )
    states = exchange(scanned)
    place = jnp.stack([lax.axis_index("head"), 1 - 2 * (lax.axis_index("pipe") & 1)]).astype(jnp.int32)
    weights = w_value.reshape(groups, step, width)
    gv_local, gain, keys_near, w_far = call(
        near_kernel,
        (pltpu.VMEM((n, width), f32), pltpu.VMEM((n, width), f32), block, pltpu.VMEM((step, width), bf16)),
        "near",
        mib=12,
        in_specs=[IN_SMEM] + [IN_HBM] * 6,
        scratch=[*small, block, block, dma((6,))],
    )(place, log_decay, segment_ids, keys, queries, out_grad, weights)

    part = pltpu.VMEM((n, step), bf16)
    near_gv, pair, single = call(
        far_kernel,
        (pltpu.VMEM((n, width), bf16), pltpu.VMEM((2, n, step), bf16), part),
        "far",
        mib=8,
        in_specs=[IN_SMEM] + [IN_VMEM] * 5 + [IN_HBM],
        scratch=[pltpu.VMEM((2, step, width), bf16), dma((2,))],
    )(place, gv_local, gain, keys_near, states, w_far, weights)

    def products(wanted, gv, name, writes):
        count = len(wanted)
        extra = (jax.ShapeDtypeStruct((n, width), bf16),) if writes else ()
        return call(
            lambda *refs: partial_kernel(wanted, *refs),
            (pltpu.VMEM((count, n, step), bf16), *extra),
            name,
            mib=4 * count,
            in_specs=[IN_SMEM, IN_VMEM, IN_HBM],
            out_specs=(IN_VMEM, *(IN_HBM for _ in extra)),
            scratch=[pltpu.VMEM((count, step, width), bf16), dma((count + 1,))],
        )(place, gv, weights)

    (soon,) = products(SOON, near_gv, "partial_soon", False)
    grad_query, grad_key = call(
        query_key_kernel,
        (jax.ShapeDtypeStruct((n, width), bf16), jax.ShapeDtypeStruct((n, width), bf16)),
        "query_key",
        mib=12,
        in_specs=[IN_HBM] * 6 + [IN_VMEM] * 2,
        scratch=[*small, block, block, block, block, dma((6,))],
    )(log_decay, segment_ids, queries, keys, values, out_grad, states, gain)

    sections = lax.axis_size("pipe")

    def hop(array, distance):
        pairs = []
        for i in range(groups):
            for c in range(sections):
                to = (i + (distance if c % 2 == 0 else -distance)) % groups
                pairs.append((i * sections + c, to * sections + c))
        return lax.ppermute(array, ("head", "pipe"), pairs)

    def add(partials, own, picks, name, *arrived):
        return call(lambda *refs: add_kernel(own, picks, *refs), part, name)(partials, *arrived)

    pair_got = hop(pair, -1)
    single_got = hop(single, 1)
    long = add(soon, 0, (0,), "add_long", pair_got)
    short = add(soon, 1, (None,), "add_short", single_got)
    long, short, near_gv = lax.optimization_barrier((long, short, near_gv))
    later, grad_value = products(LATER, near_gv, "partial_later", True)
    long_got = hop(long, -2)
    short_got = hop(short, 1)
    long = add(later, 0, (1, None), "add_long_last", pair_got, long_got)
    short = add(later, 1, (None,), "add_short_last", short_got)
    long, short, grad_query, grad_key = lax.optimization_barrier((long, short, grad_query, grad_key))
    long_got = hop(long, -1)
    short_got = hop(short, 1)
    summed = add(later, 2, (None, None), "add_last", long_got, short_got)
    shifted = lax.ppermute(summed, "pipe", [((i + 1) % sections, i) for i in range(sections)])
    return (grad_query[None], grad_key[None], grad_value[None], shifted[None])


def solution(mesh):
    ctx, head, pipe = (mesh.shape[name] for name in ("ctx", "head", "pipe"))
    grid = Mesh(np.asarray(mesh.devices).reshape(ctx // ROW, ROW, head, pipe), ("plane", "line", "head", "pipe"))
    seq = ("plane", "line")
    tokens = P("pipe", seq, "head")
    return jax.shard_map(
        body,
        mesh=grid,
        in_specs=(tokens, tokens, tokens, tokens, P("pipe", "head", seq), P("pipe", seq), P("pipe", None, "head")),
        out_specs=(tokens, tokens, tokens, tokens),
        check_vma=False,
    )
```

```python
import jax
import jax.numpy as jnp
import numpy as np
from jax import lax
from jax.experimental import pallas as pl
from jax.experimental.pallas import tpu as pltpu
from jax.sharding import Mesh
from jax.sharding import PartitionSpec as P

f32, bf16 = jnp.float32, jnp.bfloat16
HIGHEST = lax.Precision.HIGHEST
ROW = 8
META = 16
NEVER = -1e30


def dot(a, b, dims):
    return lax.dot_general(a, b, (dims, ((), ())), preferred_element_type=f32)


def iota2(n, axis):
    return lax.broadcasted_iota(jnp.int32, (n, n), axis)


def cumulative_columns(rates):
    n = rates.shape[1]
    lower = (iota2(n, 1) <= iota2(n, 0)).astype(f32)
    return lax.dot_general(lower, rates, (((1,), (1,)), ((), ())), precision=HIGHEST, preferred_element_type=f32)


def cumulative_rows(rates):
    n = rates.shape[1]
    upper = (iota2(n, 0) <= iota2(n, 1)).astype(f32)
    return lax.dot_general(rates, upper, (((1,), (0,)), ((), ())), precision=HIGHEST, preferred_element_type=f32)


def write_message(out, h, states, first, last, through, width):
    share = states[0].shape[0] // 2
    high = through.astype(bf16)
    low = (through - high.astype(f32)).astype(bf16)
    row = lax.broadcasted_iota(jnp.int32, (META, width), 0)
    meta = jnp.where(row == 0, first, jnp.where(row == 1, last, 0.0))
    meta = jnp.where(row == 2, high.astype(f32), jnp.where(row == 3, low.astype(f32), meta)).astype(bf16)
    for half in range(2):
        p = 2 * h + half
        for i, state in enumerate(states):
            out[p, i * share : (i + 1) * share, :] = state[half * share : (half + 1) * share].astype(bf16)
        out[p, 2 * share : 2 * share + META, :] = meta


def ids_column(seg_row):
    n = seg_row.shape[1]
    on_diagonal = iota2(n, 0) == iota2(n, 1)
    return jnp.sum(jnp.where(on_diagonal, seg_row[...].astype(f32), 0.0), axis=1, keepdims=True)


def block_ids(seg):
    n = seg.shape[0]
    return seg[0:1, :], seg[n - 1 : n, :]


def fetch(sources, targets, sems):
    copies = [pltpu.make_async_copy(src, dst, sems.at[i]) for i, (src, dst) in enumerate(zip(sources, targets))]
    for copy in copies:
        copy.start()
    return copies


def local_kernel(rates_in, seg_in, q_in, o_in, k_in, v_in, out, rates, seg_row, q, o, k, v, sems):
    sources = (rates_in, seg_in, q_in, o_in, k_in, v_in)
    rates_copy, seg_copy, *others = fetch(sources, (rates, seg_row, q, o, k, v), sems)
    rates_copy.wait()
    cum = cumulative_columns(rates[0])
    heads = rates.shape[1]
    n = cum.shape[0]
    dh = q.shape[2] // heads
    seg_copy.wait()
    seg = ids_column(seg_row)
    first, last = block_ids(seg)
    ahead = jnp.where(seg == seg[0:1, :], jnp.exp(cum), 0.0)
    behind = jnp.where(seg == seg[n - 1 : n, :], jnp.exp(cum[n - 1 : n, :] - cum), 0.0)
    for copy in others:
        copy.wait()
    for h in range(heads):
        cols = slice(h * dh, (h + 1) * dh)
        scaled_q = (q[0, :, cols].astype(f32) * ahead[:, h : h + 1]).astype(bf16)
        scaled_k = (k[0, :, cols].astype(f32) * behind[:, h : h + 1]).astype(bf16)
        states = (dot(scaled_q, o[0, :, cols], ((0,), (0,))), dot(scaled_k, v[0, :, cols], ((0,), (0,))))
        write_message(out, h, states, first, last, jnp.exp(cum[n - 1 : n, h : h + 1]), dh)


def scores(a, b, weight):
    return (dot(a, b, ((1,), (1,))) * weight).astype(bf16)


def decay_weight(cum_col, cum_row, keep):
    return jnp.exp(jnp.where(keep, cum_col - cum_row, NEVER))


def near_kernel(place, rates_in, seg_in, k_in, q_in, o_in, w_in, gv, gain, k, w, rates, seg_row, q, o, sems):
    w_pair = [w_in.at[destination(place, offset, w_in.shape[0])] for offset in PAIR]
    sources = (rates_in, seg_in, k_in, q_in, o_in, *w_pair)
    targets = (rates, seg_row, k, q, o, *(w.at[i] for i in range(len(PAIR))))
    rates_copy, seg_copy, *others = fetch(sources, targets, sems)
    others, w_copies = others[:3], others[3:]
    rates_copy.wait()
    cum = cumulative_columns(rates[0])
    cum_t = cumulative_rows(rates[0])
    heads = rates.shape[1]
    n = cum.shape[0]
    dh = q.shape[2] // heads
    seg_copy.wait()
    seg = ids_column(seg_row)
    keep = (iota2(n, 1) <= iota2(n, 0)) & (seg == seg_row[...].astype(f32))
    behind = jnp.where(seg == seg[n - 1 : n, :], jnp.exp(cum[n - 1 : n, :] - cum), 0.0)
    for copy in others:
        copy.wait()
    for h in range(heads):
        cols = slice(h * dh, (h + 1) * dh)
        weight = decay_weight(cum[:, h : h + 1], cum_t[h : h + 1, :], keep)
        ks = scores(q[0, :, cols], k[0, :, cols], weight)
        gv[:, cols] = dot(ks, o[0, :, cols], ((0,), (0,)))
        gain[:, cols] = jnp.broadcast_to(behind[:, h : h + 1], (n, dh))
    for copy in w_copies:
        copy.wait()


def unpack(msg, y, reverse):
    share = (msg.shape[1] - META) // 2
    start = 0 if reverse else share
    meta = msg[y, 2 * share : 2 * share + META, :].astype(f32)
    state = msg[y, start : start + share, :].astype(f32)
    return state, meta[0:1], meta[1:2], meta[2:3] + meta[3:4]


def order(reverse):
    return range(ROW - 1, -1, -1) if reverse else range(ROW)


def row_total_kernel(msg, out_backward, out_forward):
    for out, reverse in ((out_backward, True), (out_forward, False)):
        share = out.shape[0] - META
        tag, total = None, None
        for y in order(reverse):
            state, first, last, through = unpack(msg, y, reverse)
            if total is None:
                total = state
            else:
                same = jnp.where((first == last) & (tag == last), through, 0.0)
                total = same * total + state
            tag = first if reverse else last
        out[0:share, :] = total.astype(bf16)
        out[share:, :] = jnp.broadcast_to(tag, (META, tag.shape[1])).astype(bf16)


def row_scan_kernel(msg, carried_backward, carried_forward, out):
    for carried, reverse in ((carried_backward, True), (carried_forward, False)):
        share = carried.shape[0] - META
        start = 0 if reverse else share
        running = carried[0:share, :].astype(f32)
        tag = carried[share : share + META, :].astype(f32)[0:1]
        for y in order(reverse):
            state, first, last, through = unpack(msg, y, reverse)
            edge = last if reverse else first
            out[y, start : start + share, :] = jnp.where(edge == tag, running, 0.0).astype(bf16)
            same = jnp.where((first == last) & (tag == last), through, 0.0)
            running = same * running + state
            tag = first if reverse else last


def head_state(states, h, reverse):
    share = states.shape[1] // 2
    start = 0 if reverse else share
    return jnp.concatenate([states[2 * h + half, start : start + share, :] for half in range(2)], axis=0)


def destination(place, offset, groups):
    return lax.rem(place[0] + groups + place[1] * offset, groups)


PAIR = (-4, -2)
SINGLE = (3,)
SOON = (-3, 2, 0)
LATER = (-1, 1)


def far_kernel(place, local, gain, k, states, w, gv, pair):
    dh = states.shape[2]
    for h in range(gv.shape[1] // dh):
        cols = slice(h * dh, (h + 1) * dh)
        far = dot(k[0, :, cols], head_state(states, h, True), ((1,), (0,)))
        gv[:, cols] = (local[:, cols] + gain[:, cols] * far).astype(bf16)
    for i in range(len(PAIR)):
        pair[i] = dot(gv[...], w[i], ((1,), (1,))).astype(bf16)


def partial_kernel(wanted, place, gv, w_in, out, *rest):
    *gv_out, w, sems = rest
    groups = w_in.shape[0]
    sources = [w_in.at[destination(place, offset, groups)] for offset in wanted]
    copies = fetch(sources, [w.at[i] for i in range(len(wanted))], sems)
    for target in gv_out:
        copies.append(pltpu.make_async_copy(gv, target, sems.at[len(wanted)]))
        copies[-1].start()
    for i in range(len(wanted)):
        copies[i].wait()
        out[i] = dot(gv[...], w[i], ((1,), (1,))).astype(bf16)
    for copy in copies[len(wanted) :]:
        copy.wait()


def add_kernel(own, picks, *refs):
    partials, *arrived, out = refs
    total = partials[own].astype(f32)
    for ref, pick in zip(arrived, picks):
        total = total + (ref[...] if pick is None else ref[pick]).astype(f32)
    out[...] = total.astype(bf16)


def query_key_kernel(
    rates_in, seg_in, q_in, k_in, v_in, o_in, states, gain, dq, dk, rates, seg_row, q, k, v, o, sems
):
    sources = (rates_in, seg_in, q_in, k_in, v_in, o_in)
    for copy in fetch(sources, (rates, seg_row, q, k, v, o), sems):
        copy.wait()
    cum = cumulative_columns(rates[0])
    cum_t = cumulative_rows(rates[0])
    heads = rates.shape[1]
    n = cum.shape[0]
    dh = q.shape[2] // heads
    seg = ids_column(seg_row)
    keep = (iota2(n, 1) <= iota2(n, 0)) & (seg == seg_row[...].astype(f32))
    reach = jnp.where(seg == seg[0:1, :], jnp.exp(cum), 0.0)
    for h in range(heads):
        cols = slice(h * dh, (h + 1) * dh)
        weight = decay_weight(cum[:, h : h + 1], cum_t[h : h + 1, :], keep)
        vs = scores(o[0, :, cols], v[0, :, cols], weight)
        f = head_state(states, h, False)
        b = head_state(states, h, True)
        far_q = dot(o[0, :, cols], f, ((1,), (1,)))
        far_k = dot(v[0, :, cols], b, ((1,), (1,)))
        dq[:, cols] = (dot(vs, k[0, :, cols], ((1,), (0,))) + reach[:, h : h + 1] * far_q).astype(bf16)
        dk[:, cols] = (dot(vs, q[0, :, cols], ((0,), (0,))) + gain[:, cols] * far_k).astype(bf16)


IN_VMEM = pl.BlockSpec(memory_space=pltpu.VMEM)
IN_SMEM = pl.BlockSpec(memory_space=pltpu.SMEM)
IN_HBM = pl.BlockSpec(memory_space=pltpu.HBM)


def call(kernel, shapes, name, mib=4, in_specs=None, out_specs=IN_VMEM, scratch=()):
    def run(*args):
        specs = in_specs or [IN_VMEM] * len(args)
        args = [pltpu.with_memory_space_constraint(a, pltpu.HBM) if spec is IN_HBM else a for a, spec in zip(args, specs)]
        return pl.pallas_call(
            kernel,
            in_specs=specs,
            out_specs=jax.tree.map(lambda _: IN_VMEM, shapes) if out_specs is IN_VMEM else out_specs,
            out_shape=shapes,
            scratch_shapes=scratch,
            compiler_params=pltpu.CompilerParams(vmem_limit_bytes=mib << 20),
            name=name,
        )(*args)

    return run


def body(queries, keys, values, out_grad, log_decay, segment_ids, w_value):
    n, width = queries.shape[1:]
    heads = log_decay.shape[1]
    dh = width // heads
    planes = lax.axis_size("plane")
    groups = lax.axis_size("head")
    share = heads * dh // ROW
    step = w_value.shape[1] // groups
    block = pltpu.VMEM((1, n, width), bf16)
    small = [pltpu.VMEM(log_decay.shape, f32), pltpu.VMEM(segment_ids.shape, jnp.int32)]
    dma = pltpu.SemaphoreType.DMA

    def exchange(array):
        return lax.all_to_all(array, "line", 0, 0, tiled=True)

    sent = call(
        local_kernel,
        pltpu.VMEM((ROW, 2 * share + META, dh), bf16),
        "local",
        mib=12,
        in_specs=[IN_HBM] * 6,
        scratch=[*small, block, block, block, block, dma((6,))],
    )(log_decay, segment_ids, queries, out_grad, keys, values)
    got = exchange(sent)
    total = pltpu.VMEM((share + META, dh), bf16)
    total_backward, total_forward = call(row_total_kernel, (total, total), "row_total")(got)
    up = [(z - 1, z) for z in range(1, planes)]
    down = [(z, z - 1) for z in range(1, planes)]
    carried_backward = lax.ppermute(total_backward, "plane", down)
    carried_forward = lax.ppermute(total_forward, "plane", up)
    scanned = call(row_scan_kernel, pltpu.VMEM((ROW, 2 * share, dh), bf16), "row_scan")(
        got, carried_backward, carried_forward
    )
    states = exchange(scanned)
    place = jnp.stack([lax.axis_index("head"), 1 - 2 * (lax.axis_index("pipe") & 1)]).astype(jnp.int32)
    weights = w_value.reshape(groups, step, width)
    gv_local, gain, keys_near, w_pair = call(
        near_kernel,
        (pltpu.VMEM((n, width), f32), pltpu.VMEM((n, width), f32), block, pltpu.VMEM((len(PAIR), step, width), bf16)),
        "near",
        mib=12,
        in_specs=[IN_SMEM] + [IN_HBM] * 6,
        scratch=[*small, block, block, dma((5 + len(PAIR),))],
    )(place, log_decay, segment_ids, keys, queries, out_grad, weights)

    part = pltpu.VMEM((n, step), bf16)
    near_gv, pair = call(
        far_kernel,
        (pltpu.VMEM((n, width), bf16), pltpu.VMEM((2, n, step), bf16)),
        "far",
        in_specs=[IN_SMEM] + [IN_VMEM] * 5,
    )(place, gv_local, gain, keys_near, states, w_pair)

    def products(wanted, gv, name, writes):
        count = len(wanted)
        extra = (jax.ShapeDtypeStruct((n, width), bf16),) if writes else ()
        return call(
            lambda *refs: partial_kernel(wanted, *refs),
            (pltpu.VMEM((count, n, step), bf16), *extra),
            name,
            mib=4 * count,
            in_specs=[IN_SMEM, IN_VMEM, IN_HBM],
            out_specs=(IN_VMEM, *(IN_HBM for _ in extra)),
            scratch=[pltpu.VMEM((count, step, width), bf16), dma((count + 1,))],
        )(place, gv, weights)

    sections = lax.axis_size("pipe")

    def hop(array, distance, cross=False):
        pairs = []
        for i in range(groups):
            for c in range(sections):
                to = (i + (distance if c % 2 == 0 else -distance)) % groups
                pairs.append((i * sections + c, to * sections + (c - cross) % sections))
        return lax.ppermute(array, ("head", "pipe"), pairs)

    def add(partials, own, picks, name, *arrived):
        return call(lambda *refs: add_kernel(own, picks, *refs), part, name)(partials, *arrived)

    pair_got = hop(pair, -1)
    (single,) = products(SINGLE, near_gv, "partial_single", False)
    single_got = hop(single, 1)
    (soon,) = products(SOON, near_gv, "partial_soon", False)
    own_got = hop(soon[2:], 0, True)
    long = add(soon, 0, (0,), "add_long", pair_got)
    short = add(soon, 1, (0,), "add_short", single_got)
    long, short, near_gv, own_got = lax.optimization_barrier((long, short, near_gv, own_got))
    later, grad_value = products(LATER, near_gv, "partial_later", True)
    long_got = hop(long, -2)
    short_got = hop(short, 1)
    long = add(later, 0, (1, None), "add_long_last", pair_got, long_got)
    short = add(later, 1, (None,), "add_short_last", short_got)
    long, short, states, gain = lax.optimization_barrier((long, short, states, gain))
    sections = lax.axis_size("pipe")

    def hop(array, distance, cross=False):
        pairs = []
        for i in range(groups):
            for c in range(sections):
                to = (i + (distance if c % 2 == 0 else -distance)) % groups
                pairs.append((i * sections + c, to * sections + (c - cross) % sections))
        return lax.ppermute(array, ("head", "pipe"), pairs)

    def add(partials, own, picks, name, *arrived):
        return call(lambda *refs: add_kernel(own, picks, *refs), part, name)(partials, *arrived)

    pair_got = hop(pair, -1)
    (single,) = products(SINGLE, near_gv, "partial_single", False)
    single_got = hop(single, 1)
    (soon,) = products(SOON, near_gv, "partial_soon", False)
    own_got = hop(soon[2:], 0, True)
    long = add(soon, 0, (0,), "add_long", pair_got)
    short = add(soon, 1, (0,), "add_short", single_got)
    long, short, near_gv, own_got = lax.optimization_barrier((long, short, near_gv, own_got))
    later, grad_value = products(LATER, near_gv, "partial_later", True)
    long_got = hop(long, -2)
    short_got = hop(short, 1)
    long = add(later, 0, (1, None), "add_long_last", pair_got, long_got)
    short = add(later, 1, (None,), "add_short_last", short_got)
    long, short, states, gain = lax.optimization_barrier((long, short, states, gain))
    grad_query, grad_key = call(
        query_key_kernel,
        (jax.ShapeDtypeStruct((n, width), bf16), jax.ShapeDtypeStruct((n, width), bf16)),
        "query_key",
        mib=12,
        in_specs=[IN_HBM] * 6 + [IN_VMEM] * 2,
        scratch=[*small, block, block, block, block, dma((6,))],
    )(log_decay, segment_ids, queries, keys, values, out_grad, states, gain)
    long_got = hop(long, -1, True)
    short_got = hop(short, 1, True)
    long_got, short_got, grad_query, grad_key = lax.optimization_barrier((long_got, short_got, grad_query, grad_key))
    grad_input = call(
        lambda *refs: add_kernel(0, (None, None), *refs), jax.ShapeDtypeStruct((n, step), bf16), "add_last"
    )(own_got, long_got, short_got)
    return (grad_query[None], grad_key[None], grad_value[None], grad_input[None])


def solution(mesh):
    ctx, head, pipe = (mesh.shape[name] for name in ("ctx", "head", "pipe"))
    grid = Mesh(np.asarray(mesh.devices).reshape(ctx // ROW, ROW, head, pipe), ("plane", "line", "head", "pipe"))
    seq = ("plane", "line")
    tokens = P("pipe", seq, "head")
    return jax.shard_map(
        body,
        mesh=grid,
        in_specs=(tokens, tokens, tokens, tokens, P("pipe", "head", seq), P("pipe", seq), P("pipe", None, "head")),
        out_specs=(tokens, tokens, tokens, tokens),
        check_vma=False,
    )
```

```python
import jax
import jax.numpy as jnp
import numpy as np
from jax import lax
from jax.experimental import pallas as pl
from jax.experimental.pallas import tpu as pltpu
from jax.sharding import Mesh
from jax.sharding import PartitionSpec as P

f32, bf16 = jnp.float32, jnp.bfloat16
HIGHEST = lax.Precision.HIGHEST
ROW = 8
META = 16
NEVER = -1e30


def dot(a, b, dims):
    return lax.dot_general(a, b, (dims, ((), ())), preferred_element_type=f32)


def iota2(n, axis):
    return lax.broadcasted_iota(jnp.int32, (n, n), axis)


def cumulative_columns(rates):
    n = rates.shape[1]
    lower = (iota2(n, 1) <= iota2(n, 0)).astype(f32)
    return lax.dot_general(lower, rates, (((1,), (1,)), ((), ())), precision=HIGHEST, preferred_element_type=f32)


def cumulative_rows(rates):
    n = rates.shape[1]
    upper = (iota2(n, 0) <= iota2(n, 1)).astype(f32)
    return lax.dot_general(rates, upper, (((1,), (0,)), ((), ())), precision=HIGHEST, preferred_element_type=f32)


def write_message(out, h, states, first, last, through, width):
    share = states[0].shape[0] // 2
    high = through.astype(bf16)
    low = (through - high.astype(f32)).astype(bf16)
    row = lax.broadcasted_iota(jnp.int32, (META, width), 0)
    meta = jnp.where(row == 0, first, jnp.where(row == 1, last, 0.0))
    meta = jnp.where(row == 2, high.astype(f32), jnp.where(row == 3, low.astype(f32), meta)).astype(bf16)
    for half in range(2):
        p = 2 * h + half
        for i, state in enumerate(states):
            out[p, i * share : (i + 1) * share, :] = state[half * share : (half + 1) * share].astype(bf16)
        out[p, 2 * share : 2 * share + META, :] = meta


def ids_column(seg_row):
    n = seg_row.shape[1]
    on_diagonal = iota2(n, 0) == iota2(n, 1)
    return jnp.sum(jnp.where(on_diagonal, seg_row[...].astype(f32), 0.0), axis=1, keepdims=True)


def block_ids(seg):
    n = seg.shape[0]
    return seg[0:1, :], seg[n - 1 : n, :]


def fetch(sources, targets, sems):
    copies = [pltpu.make_async_copy(src, dst, sems.at[i]) for i, (src, dst) in enumerate(zip(sources, targets))]
    for copy in copies:
        copy.start()
    return copies


def local_kernel(rates_in, seg_in, q_in, o_in, k_in, v_in, out, rates, seg_row, q, o, k, v, sems):
    sources = (rates_in, seg_in, q_in, o_in, k_in, v_in)
    rates_copy, seg_copy, *others = fetch(sources, (rates, seg_row, q, o, k, v), sems)
    rates_copy.wait()
    cum = cumulative_columns(rates[0])
    heads = rates.shape[1]
    n = cum.shape[0]
    dh = q.shape[2] // heads
    seg_copy.wait()
    seg = ids_column(seg_row)
    first, last = block_ids(seg)
    ahead = jnp.where(seg == seg[0:1, :], jnp.exp(cum), 0.0)
    behind = jnp.where(seg == seg[n - 1 : n, :], jnp.exp(cum[n - 1 : n, :] - cum), 0.0)
    for copy in others:
        copy.wait()
    for h in range(heads):
        cols = slice(h * dh, (h + 1) * dh)
        scaled_q = (q[0, :, cols].astype(f32) * ahead[:, h : h + 1]).astype(bf16)
        scaled_k = (k[0, :, cols].astype(f32) * behind[:, h : h + 1]).astype(bf16)
        states = (dot(scaled_q, o[0, :, cols], ((0,), (0,))), dot(scaled_k, v[0, :, cols], ((0,), (0,))))
        write_message(out, h, states, first, last, jnp.exp(cum[n - 1 : n, h : h + 1]), dh)


def scores(a, b, weight):
    return (dot(a, b, ((1,), (1,))) * weight).astype(bf16)


def decay_weight(cum_col, cum_row, keep):
    return jnp.exp(jnp.where(keep, cum_col - cum_row, NEVER))


def near_kernel(place, rates_in, seg_in, k_in, q_in, o_in, w_in, gv, gain, k, w, rates, seg_row, q, o, sems):
    w_first = [w_in.at[destination(place, offset, w_in.shape[0])] for offset in FIRST]
    sources = (rates_in, seg_in, k_in, q_in, o_in, *w_first)
    targets = (rates, seg_row, k, q, o, *(w.at[i] for i in range(len(FIRST))))
    rates_copy, seg_copy, *others = fetch(sources, targets, sems)
    others, w_copies = others[:3], others[3:]
    rates_copy.wait()
    cum = cumulative_columns(rates[0])
    cum_t = cumulative_rows(rates[0])
    heads = rates.shape[1]
    n = cum.shape[0]
    dh = q.shape[2] // heads
    seg_copy.wait()
    seg = ids_column(seg_row)
    keep = (iota2(n, 1) <= iota2(n, 0)) & (seg == seg_row[...].astype(f32))
    behind = jnp.where(seg == seg[n - 1 : n, :], jnp.exp(cum[n - 1 : n, :] - cum), 0.0)
    for copy in others:
        copy.wait()
    for h in range(heads):
        cols = slice(h * dh, (h + 1) * dh)
        weight = decay_weight(cum[:, h : h + 1], cum_t[h : h + 1, :], keep)
        ks = scores(q[0, :, cols], k[0, :, cols], weight)
        gv[:, cols] = dot(ks, o[0, :, cols], ((0,), (0,)))
    gain[...] = jnp.pad(behind, ((0, 0), (0, gain.shape[1] - heads)))
    for copy in w_copies:
        copy.wait()


def unpack(msg, y, reverse):
    share = (msg.shape[1] - META) // 2
    start = 0 if reverse else share
    meta = msg[y, 2 * share : 2 * share + META, :].astype(f32)
    state = msg[y, start : start + share, :].astype(f32)
    return state, meta[0:1], meta[1:2], meta[2:3] + meta[3:4]


def order(reverse):
    return range(ROW - 1, -1, -1) if reverse else range(ROW)


def row_total_kernel(msg, out_backward, out_forward):
    for out, reverse in ((out_backward, True), (out_forward, False)):
        share = out.shape[0] - META
        tag, total = None, None
        for y in order(reverse):
            state, first, last, through = unpack(msg, y, reverse)
            if total is None:
                total = state
            else:
                same = jnp.where((first == last) & (tag == last), through, 0.0)
                total = same * total + state
            tag = first if reverse else last
        out[0:share, :] = total.astype(bf16)
        out[share:, :] = jnp.broadcast_to(tag, (META, tag.shape[1])).astype(bf16)


def row_scan_kernel(msg, carried_backward, carried_forward, out):
    for carried, reverse in ((carried_backward, True), (carried_forward, False)):
        share = carried.shape[0] - META
        start = 0 if reverse else share
        running = carried[0:share, :].astype(f32)
        tag = carried[share : share + META, :].astype(f32)[0:1]
        for y in order(reverse):
            state, first, last, through = unpack(msg, y, reverse)
            edge = last if reverse else first
            out[y, start : start + share, :] = jnp.where(edge == tag, running, 0.0).astype(bf16)
            same = jnp.where((first == last) & (tag == last), through, 0.0)
            running = same * running + state
            tag = first if reverse else last


def head_state(states, h, reverse):
    share = states.shape[1] // 2
    start = 0 if reverse else share
    return jnp.concatenate([states[2 * h + half, start : start + share, :] for half in range(2)], axis=0)


def destination(place, offset, groups):
    return lax.rem(place[0] + groups + place[1] * offset, groups)


FIRST = (-4, -2, 3)
SOON = (-3, 2)
LATER = (-1, 1, 0)


def far_kernel(local, gain, k, states, w, gv, pair, single):
    dh = states.shape[2]
    for h in range(gv.shape[1] // dh):
        cols = slice(h * dh, (h + 1) * dh)
        far = dot(k[0, :, cols], head_state(states, h, True), ((1,), (0,)))
        gv[:, cols] = (local[:, cols] + gain[:, h : h + 1] * far).astype(bf16)
    for i in range(pair.shape[0]):
        pair[i] = dot(gv[...], w[i], ((1,), (1,))).astype(bf16)
    single[...] = dot(gv[...], w[pair.shape[0]], ((1,), (1,))).astype(bf16)


def partial_kernel(wanted, place, gv, w_in, out, *rest):
    *gv_out, w, sems = rest
    groups = w_in.shape[0]
    sources = [w_in.at[destination(place, offset, groups)] for offset in wanted]
    copies = fetch(sources, [w.at[i] for i in range(len(wanted))], sems)
    for target in gv_out:
        copies.append(pltpu.make_async_copy(gv, target, sems.at[len(wanted)]))
        copies[-1].start()
    for i in range(len(wanted)):
        copies[i].wait()
        out[i] = dot(gv[...], w[i], ((1,), (1,))).astype(bf16)
    for copy in copies[len(wanted) :]:
        copy.wait()


def add_kernel(own, picks, *refs):
    partials, *arrived, out = refs
    total = partials[own].astype(f32)
    for ref, pick in zip(arrived, picks):
        total = total + (ref[...] if pick is None else ref[pick]).astype(f32)
    out[...] = total.astype(bf16)


def query_key_kernel(
    rates_in, seg_in, q_in, k_in, v_in, o_in, states, gain, dq, dk, rates, seg_row, q, k, v, o, sems
):
    sources = (rates_in, seg_in, q_in, k_in, v_in, o_in)
    for copy in fetch(sources, (rates, seg_row, q, k, v, o), sems):
        copy.wait()
    cum = cumulative_columns(rates[0])
    cum_t = cumulative_rows(rates[0])
    heads = rates.shape[1]
    n = cum.shape[0]
    dh = q.shape[2] // heads
    seg = ids_column(seg_row)
    keep = (iota2(n, 1) <= iota2(n, 0)) & (seg == seg_row[...].astype(f32))
    reach = jnp.where(seg == seg[0:1, :], jnp.exp(cum), 0.0)
    for h in range(heads):
        cols = slice(h * dh, (h + 1) * dh)
        weight = decay_weight(cum[:, h : h + 1], cum_t[h : h + 1, :], keep)
        vs = scores(o[0, :, cols], v[0, :, cols], weight)
        f = head_state(states, h, False)
        b = head_state(states, h, True)
        far_q = dot(o[0, :, cols], f, ((1,), (1,)))
        far_k = dot(v[0, :, cols], b, ((1,), (1,)))
        dq[:, cols] = (dot(vs, k[0, :, cols], ((1,), (0,))) + reach[:, h : h + 1] * far_q).astype(bf16)
        dk[:, cols] = (dot(vs, q[0, :, cols], ((0,), (0,))) + gain[:, h : h + 1] * far_k).astype(bf16)


IN_VMEM = pl.BlockSpec(memory_space=pltpu.VMEM)
IN_SMEM = pl.BlockSpec(memory_space=pltpu.SMEM)
IN_HBM = pl.BlockSpec(memory_space=pltpu.HBM)


def call(kernel, shapes, name, mib=4, in_specs=None, out_specs=IN_VMEM, scratch=()):
    def run(*args):
        specs = in_specs or [IN_VMEM] * len(args)
        args = [pltpu.with_memory_space_constraint(a, pltpu.HBM) if spec is IN_HBM else a for a, spec in zip(args, specs)]
        return pl.pallas_call(
            kernel,
            in_specs=specs,
            out_specs=jax.tree.map(lambda _: IN_VMEM, shapes) if out_specs is IN_VMEM else out_specs,
            out_shape=shapes,
            scratch_shapes=scratch,
            compiler_params=pltpu.CompilerParams(vmem_limit_bytes=mib << 20),
            name=name,
        )(*args)

    return run


def body(queries, keys, values, out_grad, log_decay, segment_ids, w_value):
    n, width = queries.shape[1:]
    heads = log_decay.shape[1]
    dh = width // heads
    planes = lax.axis_size("plane")
    groups = lax.axis_size("head")
    share = heads * dh // ROW
    step = w_value.shape[1] // groups
    block = pltpu.VMEM((1, n, width), bf16)
    small = [pltpu.VMEM(log_decay.shape, f32), pltpu.VMEM(segment_ids.shape, jnp.int32)]
    dma = pltpu.SemaphoreType.DMA

    def exchange(array):
        return lax.all_to_all(array, "line", 0, 0, tiled=True)

    sent = call(
        local_kernel,
        pltpu.VMEM((ROW, 2 * share + META, dh), bf16),
        "local",
        mib=12,
        in_specs=[IN_HBM] * 6,
        scratch=[*small, block, block, block, block, dma((6,))],
    )(log_decay, segment_ids, queries, out_grad, keys, values)
    got = exchange(sent)
    total = pltpu.VMEM((share + META, dh), bf16)
    total_backward, total_forward = call(row_total_kernel, (total, total), "row_total")(got)
    up = [(z - 1, z) for z in range(1, planes)]
    down = [(z, z - 1) for z in range(1, planes)]
    carried_backward = lax.ppermute(total_backward, "plane", down)
    carried_forward = lax.ppermute(total_forward, "plane", up)
    scanned = call(row_scan_kernel, pltpu.VMEM((ROW, 2 * share, dh), bf16), "row_scan")(
        got, carried_backward, carried_forward
    )
    states = exchange(scanned)
    place = jnp.stack([lax.axis_index("head"), 1 - 2 * (lax.axis_index("pipe") & 1)]).astype(jnp.int32)
    weights = w_value.reshape(groups, step, width)
    gv_local, gain, keys_near, w_first = call(
        near_kernel,
        (pltpu.VMEM((n, width), f32), pltpu.VMEM((n, dh), f32), block, pltpu.VMEM((len(FIRST), step, width), bf16)),
        "near",
        mib=12,
        in_specs=[IN_SMEM] + [IN_HBM] * 6,
        scratch=[*small, block, block, dma((5 + len(FIRST),))],
    )(place, log_decay, segment_ids, keys, queries, out_grad, weights)

    part = pltpu.VMEM((n, step), bf16)
    near_gv, pair, single = call(
        far_kernel, (pltpu.VMEM((n, width), bf16), pltpu.VMEM((2, n, step), bf16), part), "far"
    )(gv_local, gain, keys_near, states, w_first)

    def products(wanted, gv, name, writes):
        count = len(wanted)
        extra = (jax.ShapeDtypeStruct((n, width), bf16),) if writes else ()
        return call(
            lambda *refs: partial_kernel(wanted, *refs),
            (pltpu.VMEM((count, n, step), bf16), *extra),
            name,
            mib=4 * count,
            in_specs=[IN_SMEM, IN_VMEM, IN_HBM],
            out_specs=(IN_VMEM, *(IN_HBM for _ in extra)),
            scratch=[pltpu.VMEM((count, step, width), bf16), dma((count + 1,))],
        )(place, gv, weights)

    sections = lax.axis_size("pipe")

    def hop(array, distance, cross=False):
        pairs = []
        for i in range(groups):
            for c in range(sections):
                to = (i + (distance if c % 2 == 0 else -distance)) % groups
                pairs.append((i * sections + c, to * sections + (c - cross) % sections))
        return lax.ppermute(array, ("head", "pipe"), pairs)

    def add(partials, own, picks, name, *arrived):
        return call(lambda *refs: add_kernel(own, picks, *refs), part, name)(partials, *arrived)

    pair_got = hop(pair, -1)
    single_got = hop(single, 1)
    (soon,) = products(SOON, near_gv, "partial_soon", False)
    long = add(soon, 0, (0,), "add_long", pair_got)
    short = add(soon, 1, (None,), "add_short", single_got)
    long, short, near_gv = lax.optimization_barrier((long, short, near_gv))
    later, grad_value = products(LATER, near_gv, "partial_later", True)
    long_got = hop(long, -2)
    short_got = hop(short, 1)
    long = add(later, 0, (1, None), "add_long_last", pair_got, long_got)
    short = add(later, 1, (None,), "add_short_last", short_got)
    long, short, own, states, gain = lax.optimization_barrier((long, short, later[2:], states, gain))
    sections = lax.axis_size("pipe")

    def hop(array, distance, cross=False):
        pairs = []
        for i in range(groups):
            for c in range(sections):
                to = (i + (distance if c % 2 == 0 else -distance)) % groups
                pairs.append((i * sections + c, to * sections + (c - cross) % sections))
        return lax.ppermute(array, ("head", "pipe"), pairs)

    def add(partials, own, picks, name, *arrived):
        return call(lambda *refs: add_kernel(own, picks, *refs), part, name)(partials, *arrived)

    pair_got = hop(pair, -1)
    single_got = hop(single, 1)
    (soon,) = products(SOON, near_gv, "partial_soon", False)
    long = add(soon, 0, (0,), "add_long", pair_got)
    short = add(soon, 1, (None,), "add_short", single_got)
    long, short, near_gv = lax.optimization_barrier((long, short, near_gv))
    later, grad_value = products(LATER, near_gv, "partial_later", True)
    long_got = hop(long, -2)
    short_got = hop(short, 1)
    long = add(later, 0, (1, None), "add_long_last", pair_got, long_got)
    short = add(later, 1, (None,), "add_short_last", short_got)
    long, short, own, states, gain = lax.optimization_barrier((long, short, later[2:], states, gain))
    grad_query, grad_key = call(
        query_key_kernel,
        (jax.ShapeDtypeStruct((n, width), bf16), jax.ShapeDtypeStruct((n, width), bf16)),
        "query_key",
        mib=12,
        in_specs=[IN_HBM] * 6 + [IN_VMEM] * 2,
        scratch=[*small, block, block, block, block, dma((6,))],
    )(log_decay, segment_ids, queries, keys, values, out_grad, states, gain)
    long_got = hop(long, -1, True)
    short_got = hop(short, 1, True)
    own_got = hop(own, 0, True)
    long_got, short_got, grad_query, grad_key = lax.optimization_barrier((long_got, short_got, grad_query, grad_key))
    grad_input = call(
        lambda *refs: add_kernel(0, (None, None), *refs), jax.ShapeDtypeStruct((n, step), bf16), "add_last"
    )(own_got, long_got, short_got)
    return (grad_query[None], grad_key[None], grad_value[None], grad_input[None])


def solution(mesh):
    ctx, head, pipe = (mesh.shape[name] for name in ("ctx", "head", "pipe"))
    grid = Mesh(np.asarray(mesh.devices).reshape(ctx // ROW, ROW, head, pipe), ("plane", "line", "head", "pipe"))
    seq = ("plane", "line")
    tokens = P("pipe", seq, "head")
    return jax.shard_map(
        body,
        mesh=grid,
        in_specs=(tokens, tokens, tokens, tokens, P("pipe", "head", seq), P("pipe", seq), P("pipe", None, "head")),
        out_specs=(tokens, tokens, tokens, tokens),
        check_vma=False,
    )
```

```python
import jax
import jax.numpy as jnp
import numpy as np
from jax import lax
from jax.experimental import pallas as pl
from jax.experimental.pallas import tpu as pltpu
from jax.sharding import Mesh
from jax.sharding import PartitionSpec as P

f32, bf16 = jnp.float32, jnp.bfloat16
HIGHEST = lax.Precision.HIGHEST
ROW = 8
META = 16
NEVER = -1e30


def dot(a, b, dims):
    return lax.dot_general(a, b, (dims, ((), ())), preferred_element_type=f32)


def iota2(n, axis):
    return lax.broadcasted_iota(jnp.int32, (n, n), axis)


def cumulative_columns(rates):
    n = rates.shape[1]
    lower = (iota2(n, 1) <= iota2(n, 0)).astype(f32)
    return lax.dot_general(lower, rates, (((1,), (1,)), ((), ())), precision=HIGHEST, preferred_element_type=f32)


def cumulative_rows(rates):
    n = rates.shape[1]
    upper = (iota2(n, 0) <= iota2(n, 1)).astype(f32)
    return lax.dot_general(rates, upper, (((1,), (0,)), ((), ())), precision=HIGHEST, preferred_element_type=f32)


def write_message(out, piece, state, entry, leave, through, width):
    rows = state.shape[0]
    high = through.astype(bf16)
    low = (through - high.astype(f32)).astype(bf16)
    row = lax.broadcasted_iota(jnp.int32, (META, width), 0)
    meta = jnp.where(row == 0, entry, jnp.where(row == 1, leave, 0.0))
    meta = jnp.where(row == 2, high.astype(f32), jnp.where(row == 3, low.astype(f32), meta)).astype(bf16)
    out[piece, 0:rows, :] = state.astype(bf16)
    out[piece, rows : rows + META, :] = meta


def ids_column(seg_row):
    n = seg_row.shape[1]
    on_diagonal = iota2(n, 0) == iota2(n, 1)
    return jnp.sum(jnp.where(on_diagonal, seg_row[...].astype(f32), 0.0), axis=1, keepdims=True)


def block_ids(seg):
    n = seg.shape[0]
    return seg[0:1, :], seg[n - 1 : n, :]


def fetch(sources, targets, sems):
    copies = [pltpu.make_async_copy(src, dst, sems.at[i]) for i, (src, dst) in enumerate(zip(sources, targets))]
    for copy in copies:
        copy.start()
    return copies


def local_kernel(_, rates_in, seg_in, q_in, o_in, k_in, v_in, out, rates, seg_row, q, o, k, v, sems):
    sources = (rates_in, seg_in, q_in, o_in, k_in, v_in)
    rates_copy, seg_copy, *others = fetch(sources, (rates, seg_row, q, o, k, v), sems)
    rates_copy.wait()
    cum = cumulative_columns(rates[0])
    heads = rates.shape[1]
    n = cum.shape[0]
    dh = q.shape[2] // heads
    seg_copy.wait()
    seg = ids_column(seg_row)
    first, last = block_ids(seg)
    ahead = jnp.where(seg == seg[0:1, :], jnp.exp(cum), 0.0)
    behind = jnp.where(seg == seg[n - 1 : n, :], jnp.exp(cum[n - 1 : n, :] - cum), 0.0)
    for copy in others:
        copy.wait()
    for h in range(heads):
        cols = slice(h * dh, (h + 1) * dh)
        scaled_q = (q[0, :, cols].astype(f32) * ahead[:, h : h + 1]).astype(bf16)
        scaled_k = (k[0, :, cols].astype(f32) * behind[:, h : h + 1]).astype(bf16)
        through = jnp.exp(cum[n - 1 : n, h : h + 1])
        write_message(out, h, dot(scaled_q, o[0, :, cols], ((0,), (0,))), last, first, through, dh)
        write_message(out, heads + h, dot(scaled_k, v[0, :, cols], ((0,), (0,))), first, last, through, dh)


def scores(a, b, weight):
    return (dot(a, b, ((1,), (1,))) * weight).astype(bf16)


def decay_weight(cum_col, cum_row, keep):
    return jnp.exp(jnp.where(keep, cum_col - cum_row, NEVER))


def near_kernel(place, rates_in, seg_in, k_in, q_in, o_in, w_in, gv, gain, k, w, rates, seg_row, q, o, sems):
    w_first = [w_in.at[destination(place, offset, w_in.shape[0])] for offset in FIRST]
    sources = (rates_in, seg_in, k_in, q_in, o_in, *w_first)
    targets = (rates, seg_row, k, q, o, *(w.at[i] for i in range(len(FIRST))))
    rates_copy, seg_copy, *others = fetch(sources, targets, sems)
    others, w_copies = others[:3], others[3:]
    rates_copy.wait()
    cum = cumulative_columns(rates[0])
    cum_t = cumulative_rows(rates[0])
    heads = rates.shape[1]
    n = cum.shape[0]
    dh = q.shape[2] // heads
    seg_copy.wait()
    seg = ids_column(seg_row)
    keep = (iota2(n, 1) <= iota2(n, 0)) & (seg == seg_row[...].astype(f32))
    behind = jnp.where(seg == seg[n - 1 : n, :], jnp.exp(cum[n - 1 : n, :] - cum), 0.0)
    for copy in others:
        copy.wait()
    for h in range(heads):
        cols = slice(h * dh, (h + 1) * dh)
        weight = decay_weight(cum[:, h : h + 1], cum_t[h : h + 1, :], keep)
        ks = scores(q[0, :, cols], k[0, :, cols], weight)
        gv[:, cols] = dot(ks, o[0, :, cols], ((0,), (0,)))
    gain[...] = jnp.pad(behind, ((0, 0), (0, gain.shape[1] - heads)))
    for copy in w_copies:
        copy.wait()


def unpack(msg, y):
    rows = msg.shape[1] - META
    block = msg[y].astype(f32)
    meta = block[rows:]
    return block[:rows], meta[0:1], meta[1:2], meta[2:3] + meta[3:4]


def block_at(place, k):
    return jnp.where(place[2] > 0, ROW - 1 - k, k)


def row_total_kernel(place, msg, out):
    rows = out.shape[0] - META
    total, _, tag, _ = unpack(msg, block_at(place, 0))
    for k in range(1, ROW):
        state, entry, leave, through = unpack(msg, block_at(place, k))
        same = jnp.where((entry == leave) & (tag == entry), through, 0.0)
        total = same * total + state
        tag = leave
    out[0:rows, :] = total.astype(bf16)
    out[rows:, :] = jnp.broadcast_to(tag, (META, tag.shape[1])).astype(bf16)


def row_scan_kernel(place, msg, carried, out):
    rows = carried.shape[0] - META
    running = carried[0:rows, :].astype(f32)
    tag = carried[rows : rows + META, :].astype(f32)[0:1]
    for k in range(ROW):
        y = block_at(place, k)
        state, entry, leave, through = unpack(msg, y)
        out[y] = jnp.where(entry == tag, running, 0.0).astype(bf16)
        same = jnp.where((entry == leave) & (tag == entry), through, 0.0)
        running = same * running + state
        tag = leave


def destination(place, offset, groups):
    return lax.rem(place[0] + groups + place[1] * offset, groups)


FIRST = (-4, -2, 3)
SOON = (-3, 2)
LATER = (-1, 1, 0)


def far_kernel(local, gain, k, states, w, gv, pair, single):
    dh = states.shape[2]
    for h in range(gv.shape[1] // dh):
        cols = slice(h * dh, (h + 1) * dh)
        far = dot(k[0, :, cols], states[h], ((1,), (0,)))
        gv[:, cols] = (local[:, cols] + gain[:, h : h + 1] * far).astype(bf16)
    for i in range(pair.shape[0]):
        pair[i] = dot(gv[...], w[i], ((1,), (1,))).astype(bf16)
    single[...] = dot(gv[...], w[pair.shape[0]], ((1,), (1,))).astype(bf16)


def partial_kernel(wanted, place, gv, w_in, out, *rest):
    *gv_out, w, sems = rest
    groups = w_in.shape[0]
    sources = [w_in.at[destination(place, offset, groups)] for offset in wanted]
    copies = fetch(sources, [w.at[i] for i in range(len(wanted))], sems)
    for target in gv_out:
        copies.append(pltpu.make_async_copy(gv, target, sems.at[len(wanted)]))
        copies[-1].start()
    for i in range(len(wanted)):
        copies[i].wait()
        out[i] = dot(gv[...], w[i], ((1,), (1,))).astype(bf16)
    for copy in copies[len(wanted) :]:
        copy.wait()


def add_kernel(own, picks, *refs):
    partials, *arrived, out = refs
    total = partials[own].astype(f32)
    for ref, pick in zip(arrived, picks):
        total = total + (ref[...] if pick is None else ref[pick]).astype(f32)
    out[...] = total.astype(bf16)


def query_key_kernel(
    rates_in, seg_in, q_in, k_in, v_in, o_in, states, gain, dq, dk, rates, seg_row, q, k, v, o, sems
):
    sources = (rates_in, seg_in, q_in, k_in, v_in, o_in)
    for copy in fetch(sources, (rates, seg_row, q, k, v, o), sems):
        copy.wait()
    cum = cumulative_columns(rates[0])
    cum_t = cumulative_rows(rates[0])
    heads = rates.shape[1]
    n = cum.shape[0]
    dh = q.shape[2] // heads
    seg = ids_column(seg_row)
    keep = (iota2(n, 1) <= iota2(n, 0)) & (seg == seg_row[...].astype(f32))
    reach = jnp.where(seg == seg[0:1, :], jnp.exp(cum), 0.0)
    for h in range(heads):
        cols = slice(h * dh, (h + 1) * dh)
        weight = decay_weight(cum[:, h : h + 1], cum_t[h : h + 1, :], keep)
        vs = scores(o[0, :, cols], v[0, :, cols], weight)
        f = states[heads + h]
        b = states[h]
        far_q = dot(o[0, :, cols], f, ((1,), (1,)))
        far_k = dot(v[0, :, cols], b, ((1,), (1,)))
        dq[:, cols] = (dot(vs, k[0, :, cols], ((1,), (0,))) + reach[:, h : h + 1] * far_q).astype(bf16)
        dk[:, cols] = (dot(vs, q[0, :, cols], ((0,), (0,))) + gain[:, h : h + 1] * far_k).astype(bf16)


IN_VMEM = pl.BlockSpec(memory_space=pltpu.VMEM)
IN_SMEM = pl.BlockSpec(memory_space=pltpu.SMEM)
IN_HBM = pl.BlockSpec(memory_space=pltpu.HBM)


def call(kernel, shapes, name, mib=4, in_specs=None, out_specs=IN_VMEM, scratch=()):
    def run(*args):
        specs = in_specs or [IN_VMEM] * len(args)
        args = [pltpu.with_memory_space_constraint(a, pltpu.HBM) if spec is IN_HBM else a for a, spec in zip(args, specs)]
        return pl.pallas_call(
            kernel,
            in_specs=specs,
            out_specs=jax.tree.map(lambda _: IN_VMEM, shapes) if out_specs is IN_VMEM else out_specs,
            out_shape=shapes,
            scratch_shapes=scratch,
            compiler_params=pltpu.CompilerParams(vmem_limit_bytes=mib << 20),
            name=name,
        )(*args)

    return run


def body(queries, keys, values, out_grad, log_decay, segment_ids, w_value):
    n, width = queries.shape[1:]
    heads = log_decay.shape[1]
    dh = width // heads
    planes = lax.axis_size("plane")
    groups = lax.axis_size("head")
    step = w_value.shape[1] // groups
    block = pltpu.VMEM((1, n, width), bf16)
    small = [pltpu.VMEM(log_decay.shape, f32), pltpu.VMEM(segment_ids.shape, jnp.int32)]
    dma = pltpu.SemaphoreType.DMA

    def exchange(array):
        return lax.all_to_all(array, "line", 0, 0, tiled=True)

    lines = lax.axis_size("line")
    back = lines // 2
    scans_back = (lax.axis_index("line") < back).astype(jnp.int32)
    place = jnp.stack([lax.axis_index("head"), 1 - 2 * (lax.axis_index("pipe") & 1), scans_back]).astype(jnp.int32)
    sent = call(
        local_kernel,
        pltpu.VMEM((ROW, dh + META, dh), bf16),
        "local",
        mib=12,
        in_specs=[IN_SMEM] + [IN_HBM] * 6,
        scratch=[*small, block, block, block, block, dma((6,))],
    )(place, log_decay, segment_ids, queries, out_grad, keys, values)
    got = exchange(sent)
    total = call(row_total_kernel, pltpu.VMEM((dh + META, dh), bf16), "row_total", in_specs=[IN_SMEM, IN_VMEM])(
        place, got
    )
    pairs = []
    for z in range(planes):
        for y in range(lines):
            to = z - 1 if y < back else z + 1
            if 0 <= to < planes:
                pairs.append((z * lines + y, to * lines + y))
    carried = lax.ppermute(total, ("plane", "line"), pairs)
    scanned = call(
        row_scan_kernel, pltpu.VMEM((ROW, dh, dh), bf16), "row_scan", in_specs=[IN_SMEM, IN_VMEM, IN_VMEM]
    )(place, got, carried)
    states = exchange(scanned)
    weights = w_value.reshape(groups, step, width)
    gv_local, gain, keys_near, w_first = call(
        near_kernel,
        (pltpu.VMEM((n, width), f32), pltpu.VMEM((n, dh), f32), block, pltpu.VMEM((len(FIRST), step, width), bf16)),
        "near",
        mib=12,
        in_specs=[IN_SMEM] + [IN_HBM] * 6,
        scratch=[*small, block, block, dma((5 + len(FIRST),))],
    )(place, log_decay, segment_ids, keys, queries, out_grad, weights)

    part = pltpu.VMEM((n, step), bf16)
    near_gv, pair, single = call(
        far_kernel, (pltpu.VMEM((n, width), bf16), pltpu.VMEM((2, n, step), bf16), part), "far"
    )(gv_local, gain, keys_near, states, w_first)

    def products(wanted, gv, name, writes):
        count = len(wanted)
        extra = (jax.ShapeDtypeStruct((n, width), bf16),) if writes else ()
        return call(
            lambda *refs: partial_kernel(wanted, *refs),
            (pltpu.VMEM((count, n, step), bf16), *extra),
            name,
            mib=4 * count,
            in_specs=[IN_SMEM, IN_VMEM, IN_HBM],
            out_specs=(IN_VMEM, *(IN_HBM for _ in extra)),
            scratch=[pltpu.VMEM((count, step, width), bf16), dma((count + 1,))],
        )(place, gv, weights)

    sections = lax.axis_size("pipe")

    def hop(array, distance, cross=False):
        pairs = []
        for i in range(groups):
            for c in range(sections):
                to = (i + (distance if c % 2 == 0 else -distance)) % groups
                pairs.append((i * sections + c, to * sections + (c - cross) % sections))
        return lax.ppermute(array, ("head", "pipe"), pairs)

    def add(partials, own, picks, name, *arrived):
        return call(lambda *refs: add_kernel(own, picks, *refs), part, name)(partials, *arrived)

    pair_got = hop(pair, -1)
    single_got = hop(single, 1)
    (soon,) = products(SOON, near_gv, "partial_soon", False)
    long = add(soon, 0, (0,), "add_long", pair_got)
    short = add(soon, 1, (None,), "add_short", single_got)
    long, short, near_gv = lax.optimization_barrier((long, short, near_gv))
    later, grad_value = products(LATER, near_gv, "partial_later", True)
    long_got = hop(long, -2)
    short_got = hop(short, 1)
    long = add(later, 0, (1, None), "add_long_last", pair_got, long_got)
    short = add(later, 1, (None,), "add_short_last", short_got)
    long, short, own, states, gain = lax.optimization_barrier((long, short, later[2:], states, gain))
    sections = lax.axis_size("pipe")

    def hop(array, distance, cross=False):
        pairs = []
        for i in range(groups):
            for c in range(sections):
                to = (i + (distance if c % 2 == 0 else -distance)) % groups
                pairs.append((i * sections + c, to * sections + (c - cross) % sections))
        return lax.ppermute(array, ("head", "pipe"), pairs)

    def add(partials, own, picks, name, *arrived):
        return call(lambda *refs: add_kernel(own, picks, *refs), part, name)(partials, *arrived)

    pair_got = hop(pair, -1)
    single_got = hop(single, 1)
    (soon,) = products(SOON, near_gv, "partial_soon", False)
    long = add(soon, 0, (0,), "add_long", pair_got)
    short = add(soon, 1, (None,), "add_short", single_got)
    long, short, near_gv = lax.optimization_barrier((long, short, near_gv))
    later, grad_value = products(LATER, near_gv, "partial_later", True)
    long_got = hop(long, -2)
    short_got = hop(short, 1)
    long = add(later, 0, (1, None), "add_long_last", pair_got, long_got)
    short = add(later, 1, (None,), "add_short_last", short_got)
    long, short, own, states, gain = lax.optimization_barrier((long, short, later[2:], states, gain))
    grad_query, grad_key = call(
        query_key_kernel,
        (jax.ShapeDtypeStruct((n, width), bf16), jax.ShapeDtypeStruct((n, width), bf16)),
        "query_key",
        mib=12,
        in_specs=[IN_HBM] * 6 + [IN_VMEM] * 2,
        scratch=[*small, block, block, block, block, dma((6,))],
    )(log_decay, segment_ids, queries, keys, values, out_grad, states, gain)
    long_got = hop(long, -1, True)
    short_got = hop(short, 1, True)
    own_got = hop(own, 0, True)
    long_got, short_got, grad_query, grad_key = lax.optimization_barrier((long_got, short_got, grad_query, grad_key))
    grad_input = call(
        lambda *refs: add_kernel(0, (None, None), *refs), jax.ShapeDtypeStruct((n, step), bf16), "add_last"
    )(own_got, long_got, short_got)
    return (grad_query[None], grad_key[None], grad_value[None], grad_input[None])


def solution(mesh):
    ctx, head, pipe = (mesh.shape[name] for name in ("ctx", "head", "pipe"))
    grid = Mesh(np.asarray(mesh.devices).reshape(ctx // ROW, ROW, head, pipe), ("plane", "line", "head", "pipe"))
    seq = ("plane", "line")
    tokens = P("pipe", seq, "head")
    return jax.shard_map(
        body,
        mesh=grid,
        in_specs=(tokens, tokens, tokens, tokens, P("pipe", "head", seq), P("pipe", seq), P("pipe", None, "head")),
        out_specs=(tokens, tokens, tokens, tokens),
        check_vma=False,
    )
```

```python
import jax
import jax.numpy as jnp
import numpy as np
from jax import lax
from jax.experimental import pallas as pl
from jax.experimental.pallas import tpu as pltpu
from jax.sharding import Mesh
from jax.sharding import PartitionSpec as P

f32, bf16 = jnp.float32, jnp.bfloat16
HIGHEST = lax.Precision.HIGHEST
ROW = 8
META = 16
NEVER = -1e30


def dot(a, b, dims):
    return lax.dot_general(a, b, (dims, ((), ())), preferred_element_type=f32)


def iota2(n, axis):
    return lax.broadcasted_iota(jnp.int32, (n, n), axis)


def cumulative_columns(rates):
    n = rates.shape[1]
    lower = (iota2(n, 1) <= iota2(n, 0)).astype(f32)
    return lax.dot_general(lower, rates, (((1,), (1,)), ((), ())), precision=HIGHEST, preferred_element_type=f32)


def cumulative_rows(rates):
    n = rates.shape[1]
    upper = (iota2(n, 0) <= iota2(n, 1)).astype(f32)
    return lax.dot_general(rates, upper, (((1,), (0,)), ((), ())), precision=HIGHEST, preferred_element_type=f32)


def write_message(out, piece, state, entry, leave, through, width):
    rows = state.shape[0]
    high = through.astype(bf16)
    low = (through - high.astype(f32)).astype(bf16)
    row = lax.broadcasted_iota(jnp.int32, (META, width), 0)
    meta = jnp.where(row == 0, entry, jnp.where(row == 1, leave, 0.0))
    meta = jnp.where(row == 2, high.astype(f32), jnp.where(row == 3, low.astype(f32), meta)).astype(bf16)
    out[piece, 0:rows, :] = state.astype(bf16)
    out[piece, rows : rows + META, :] = meta


def ids_column(seg_row):
    n = seg_row.shape[1]
    on_diagonal = iota2(n, 0) == iota2(n, 1)
    return jnp.sum(jnp.where(on_diagonal, seg_row[...].astype(f32), 0.0), axis=1, keepdims=True)


def block_ids(seg):
    n = seg.shape[0]
    return seg[0:1, :], seg[n - 1 : n, :]


def fetch(sources, targets, sems):
    copies = [pltpu.make_async_copy(src, dst, sems.at[i]) for i, (src, dst) in enumerate(zip(sources, targets))]
    for copy in copies:
        copy.start()
    return copies


def local_kernel(rates_in, seg_in, q_in, o_in, k_in, v_in, out, rates, seg_row, q, o, k, v, sems):
    sources = (rates_in, seg_in, q_in, o_in, k_in, v_in)
    rates_copy, seg_copy, *others = fetch(sources, (rates, seg_row, q, o, k, v), sems)
    rates_copy.wait()
    cum = cumulative_columns(rates[0])
    heads = rates.shape[1]
    n = cum.shape[0]
    dh = q.shape[2] // heads
    seg_copy.wait()
    seg = ids_column(seg_row)
    first, last = block_ids(seg)
    ahead = jnp.where(seg == seg[0:1, :], jnp.exp(cum), 0.0)
    behind = jnp.where(seg == seg[n - 1 : n, :], jnp.exp(cum[n - 1 : n, :] - cum), 0.0)
    for copy in others:
        copy.wait()
    for h in range(heads):
        cols = slice(h * dh, (h + 1) * dh)
        scaled_q = (q[0, :, cols].astype(f32) * ahead[:, h : h + 1]).astype(bf16)
        scaled_k = (k[0, :, cols].astype(f32) * behind[:, h : h + 1]).astype(bf16)
        through = jnp.exp(cum[n - 1 : n, h : h + 1])
        write_message(out, h, dot(scaled_q, o[0, :, cols], ((0,), (0,))), last, first, through, dh)
        write_message(out, heads + h, dot(scaled_k, v[0, :, cols], ((0,), (0,))), first, last, through, dh)


def scores(a, b, weight):
    return (dot(a, b, ((1,), (1,))) * weight).astype(bf16)


def decay_weight(cum_col, cum_row, keep):
    return jnp.exp(jnp.where(keep, cum_col - cum_row, NEVER))


def near_kernel(rates_in, seg_in, k_in, q_in, o_in, w_in, gv, gain, k, w, rates, seg_row, q, o, sems):
    w_first = [w_in.at[destination(offset, w_in.shape[0])] for offset in FIRST]
    sources = (rates_in, seg_in, k_in, q_in, o_in, *w_first)
    targets = (rates, seg_row, k, q, o, *(w.at[i] for i in range(len(FIRST))))
    rates_copy, seg_copy, *others = fetch(sources, targets, sems)
    others, w_copies = others[:3], others[3:]
    rates_copy.wait()
    cum = cumulative_columns(rates[0])
    cum_t = cumulative_rows(rates[0])
    heads = rates.shape[1]
    n = cum.shape[0]
    dh = q.shape[2] // heads
    seg_copy.wait()
    seg = ids_column(seg_row)
    keep = (iota2(n, 1) <= iota2(n, 0)) & (seg == seg_row[...].astype(f32))
    behind = jnp.where(seg == seg[n - 1 : n, :], jnp.exp(cum[n - 1 : n, :] - cum), 0.0)
    for copy in others:
        copy.wait()
    for h in range(heads):
        cols = slice(h * dh, (h + 1) * dh)
        weight = decay_weight(cum[:, h : h + 1], cum_t[h : h + 1, :], keep)
        ks = scores(q[0, :, cols], k[0, :, cols], weight)
        gv[:, cols] = dot(ks, o[0, :, cols], ((0,), (0,)))
    gain[...] = jnp.pad(behind, ((0, 0), (0, gain.shape[1] - heads)))
    for copy in w_copies:
        copy.wait()


def unpack(msg, y):
    rows = msg.shape[1] - META
    block = msg[y].astype(f32)
    meta = block[rows:]
    return block[:rows], meta[0:1], meta[1:2], meta[2:3] + meta[3:4]


def block_at(k):
    return jnp.where(lax.axis_index("line") < ROW // 2, ROW - 1 - k, k)


def row_total_kernel(msg, out):
    rows = out.shape[0] - META
    total, _, tag, _ = unpack(msg, block_at(0))
    for k in range(1, ROW):
        state, entry, leave, through = unpack(msg, block_at(k))
        same = jnp.where((entry == leave) & (tag == entry), through, 0.0)
        total = same * total + state
        tag = leave
    out[0:rows, :] = total.astype(bf16)
    out[rows:, :] = jnp.broadcast_to(tag, (META, tag.shape[1])).astype(bf16)


def row_scan_kernel(msg, carried, out):
    rows = carried.shape[0] - META
    running = carried[0:rows, :].astype(f32)
    tag = carried[rows : rows + META, :].astype(f32)[0:1]
    for k in range(ROW):
        y = block_at(k)
        state, entry, leave, through = unpack(msg, y)
        out[y] = jnp.where(entry == tag, running, 0.0).astype(bf16)
        same = jnp.where((entry == leave) & (tag == entry), through, 0.0)
        running = same * running + state
        tag = leave


def destination(offset, groups):
    sign = 1 - 2 * (lax.axis_index("pipe") & 1)
    return lax.rem(lax.axis_index("head") + groups + sign * offset, groups)


FIRST = (-4, -2, 3)
SOON = (-3, 2)
LATER = (-1, 1, 0)


def far_kernel(local, gain, k, states, w, gv, pair, single):
    dh = states.shape[2]
    for h in range(gv.shape[1] // dh):
        cols = slice(h * dh, (h + 1) * dh)
        far = dot(k[0, :, cols], states[h], ((1,), (0,)))
        gv[:, cols] = (local[:, cols] + gain[:, h : h + 1] * far).astype(bf16)
    for i in range(pair.shape[0]):
        pair[i] = dot(gv[...], w[i], ((1,), (1,))).astype(bf16)
    single[...] = dot(gv[...], w[pair.shape[0]], ((1,), (1,))).astype(bf16)


def partial_kernel(wanted, gv, w_in, out, *rest):
    *gv_out, w, sems = rest
    groups = w_in.shape[0]
    sources = [w_in.at[destination(offset, groups)] for offset in wanted]
    copies = fetch(sources, [w.at[i] for i in range(len(wanted))], sems)
    for target in gv_out:
        copies.append(pltpu.make_async_copy(gv, target, sems.at[len(wanted)]))
        copies[-1].start()
    for i in range(len(wanted)):
        copies[i].wait()
        out[i] = dot(gv[...], w[i], ((1,), (1,))).astype(bf16)
    for copy in copies[len(wanted) :]:
        copy.wait()


def add_kernel(own, picks, *refs):
    partials, *arrived, out = refs
    total = partials[own].astype(f32)
    for ref, pick in zip(arrived, picks):
        total = total + (ref[...] if pick is None else ref[pick]).astype(f32)
    out[...] = total.astype(bf16)


def query_key_kernel(
    rates_in, seg_in, q_in, k_in, v_in, o_in, states, gain, dq, dk, rates, seg_row, q, k, v, o, sems
):
    sources = (rates_in, seg_in, q_in, k_in, v_in, o_in)
    for copy in fetch(sources, (rates, seg_row, q, k, v, o), sems):
        copy.wait()
    cum = cumulative_columns(rates[0])
    cum_t = cumulative_rows(rates[0])
    heads = rates.shape[1]
    n = cum.shape[0]
    dh = q.shape[2] // heads
    seg = ids_column(seg_row)
    keep = (iota2(n, 1) <= iota2(n, 0)) & (seg == seg_row[...].astype(f32))
    reach = jnp.where(seg == seg[0:1, :], jnp.exp(cum), 0.0)
    for h in range(heads):
        cols = slice(h * dh, (h + 1) * dh)
        weight = decay_weight(cum[:, h : h + 1], cum_t[h : h + 1, :], keep)
        vs = scores(o[0, :, cols], v[0, :, cols], weight)
        f = states[heads + h]
        b = states[h]
        far_q = dot(o[0, :, cols], f, ((1,), (1,)))
        far_k = dot(v[0, :, cols], b, ((1,), (1,)))
        dq[:, cols] = (dot(vs, k[0, :, cols], ((1,), (0,))) + reach[:, h : h + 1] * far_q).astype(bf16)
        dk[:, cols] = (dot(vs, q[0, :, cols], ((0,), (0,))) + gain[:, h : h + 1] * far_k).astype(bf16)


IN_VMEM = pl.BlockSpec(memory_space=pltpu.VMEM)
IN_HBM = pl.BlockSpec(memory_space=pltpu.HBM)


def call(kernel, shapes, name, mib=4, in_specs=None, out_specs=IN_VMEM, scratch=()):
    def run(*args):
        specs = in_specs or [IN_VMEM] * len(args)
        args = [pltpu.with_memory_space_constraint(a, pltpu.HBM) if spec is IN_HBM else a for a, spec in zip(args, specs)]
        return pl.pallas_call(
            kernel,
            in_specs=specs,
            out_specs=jax.tree.map(lambda _: IN_VMEM, shapes) if out_specs is IN_VMEM else out_specs,
            out_shape=shapes,
            scratch_shapes=scratch,
            compiler_params=pltpu.CompilerParams(vmem_limit_bytes=mib << 20),
            name=name,
        )(*args)

    return run


def body(queries, keys, values, out_grad, log_decay, segment_ids, w_value):
    n, width = queries.shape[1:]
    heads = log_decay.shape[1]
    dh = width // heads
    planes = lax.axis_size("plane")
    groups = lax.axis_size("head")
    step = w_value.shape[1] // groups
    block = pltpu.VMEM((1, n, width), bf16)
    small = [pltpu.VMEM(log_decay.shape, f32), pltpu.VMEM(segment_ids.shape, jnp.int32)]
    dma = pltpu.SemaphoreType.DMA

    def exchange(array):
        return lax.all_to_all(array, "line", 0, 0, tiled=True)

    lines = lax.axis_size("line")
    back = lines // 2
    sent = call(
        local_kernel,
        pltpu.VMEM((ROW, dh + META, dh), bf16),
        "local",
        mib=12,
        in_specs=[IN_HBM] * 6,
        scratch=[*small, block, block, block, block, dma((6,))],
    )(log_decay, segment_ids, queries, out_grad, keys, values)
    got = exchange(sent)
    total = call(row_total_kernel, pltpu.VMEM((dh + META, dh), bf16), "row_total")(got)
    pairs = []
    for z in range(planes):
        for y in range(lines):
            to = z - 1 if y < back else z + 1
            if 0 <= to < planes:
                pairs.append((z * lines + y, to * lines + y))
    carried = lax.ppermute(total, ("plane", "line"), pairs)
    scanned = call(row_scan_kernel, pltpu.VMEM((ROW, dh, dh), bf16), "row_scan")(got, carried)
    states = exchange(scanned)
    weights = w_value.reshape(groups, step, width)
    gv_local, gain, keys_near, w_first = call(
        near_kernel,
        (pltpu.VMEM((n, width), f32), pltpu.VMEM((n, dh), f32), block, pltpu.VMEM((len(FIRST), step, width), bf16)),
        "near",
        mib=12,
        in_specs=[IN_HBM] * 6,
        scratch=[*small, block, block, dma((5 + len(FIRST),))],
    )(log_decay, segment_ids, keys, queries, out_grad, weights)

    part = pltpu.VMEM((n, step), bf16)
    near_gv, pair, single = call(
        far_kernel, (pltpu.VMEM((n, width), bf16), pltpu.VMEM((2, n, step), bf16), part), "far"
    )(gv_local, gain, keys_near, states, w_first)

    def products(wanted, gv, name, writes):
        count = len(wanted)
        extra = (jax.ShapeDtypeStruct((n, width), bf16),) if writes else ()
        return call(
            lambda *refs: partial_kernel(wanted, *refs),
            (pltpu.VMEM((count, n, step), bf16), *extra),
            name,
            mib=4 * count,
            in_specs=[IN_VMEM, IN_HBM],
            out_specs=(IN_VMEM, *(IN_HBM for _ in extra)),
            scratch=[pltpu.VMEM((count, step, width), bf16), dma((count + 1,))],
        )(gv, weights)

    sections = lax.axis_size("pipe")

    def hop(array, distance, cross=False):
        pairs = []
        for i in range(groups):
            for c in range(sections):
                to = (i + (distance if c % 2 == 0 else -distance)) % groups
                pairs.append((i * sections + c, to * sections + (c - cross) % sections))
        return lax.ppermute(array, ("head", "pipe"), pairs)

    def add(partials, own, picks, name, *arrived):
        return call(lambda *refs: add_kernel(own, picks, *refs), part, name)(partials, *arrived)

    pair_got = hop(pair, -1)
    single_got = hop(single, 1)
    (soon,) = products(SOON, near_gv, "partial_soon", False)
    long = add(soon, 0, (0,), "add_long", pair_got)
    short = add(soon, 1, (None,), "add_short", single_got)
    long, short, near_gv = lax.optimization_barrier((long, short, near_gv))
    later, grad_value = products(LATER, near_gv, "partial_later", True)
    long_got = hop(long, -2)
    short_got = hop(short, 1)
    long = add(later, 0, (1, None), "add_long_last", pair_got, long_got)
    short = add(later, 1, (None,), "add_short_last", short_got)
    long, short, own, states, gain = lax.optimization_barrier((long, short, later[2:], states, gain))
    sections = lax.axis_size("pipe")

    def hop(array, distance, cross=False):
        pairs = []
        for i in range(groups):
            for c in range(sections):
                to = (i + (distance if c % 2 == 0 else -distance)) % groups
                pairs.append((i * sections + c, to * sections + (c - cross) % sections))
        return lax.ppermute(array, ("head", "pipe"), pairs)

    def add(partials, own, picks, name, *arrived):
        return call(lambda *refs: add_kernel(own, picks, *refs), part, name)(partials, *arrived)

    pair_got = hop(pair, -1)
    single_got = hop(single, 1)
    (soon,) = products(SOON, near_gv, "partial_soon", False)
    long = add(soon, 0, (0,), "add_long", pair_got)
    short = add(soon, 1, (None,), "add_short", single_got)
    long, short, near_gv = lax.optimization_barrier((long, short, near_gv))
    later, grad_value = products(LATER, near_gv, "partial_later", True)
    long_got = hop(long, -2)
    short_got = hop(short, 1)
    long = add(later, 0, (1, None), "add_long_last", pair_got, long_got)
    short = add(later, 1, (None,), "add_short_last", short_got)
    long, short, own, states, gain = lax.optimization_barrier((long, short, later[2:], states, gain))
    grad_query, grad_key = call(
        query_key_kernel,
        (jax.ShapeDtypeStruct((n, width), bf16), jax.ShapeDtypeStruct((n, width), bf16)),
        "query_key",
        mib=12,
        in_specs=[IN_HBM] * 6 + [IN_VMEM] * 2,
        scratch=[*small, block, block, block, block, dma((6,))],
    )(log_decay, segment_ids, queries, keys, values, out_grad, states, gain)
    long_got = hop(long, -1, True)
    short_got = hop(short, 1, True)
    own_got = hop(own, 0, True)
    long_got, short_got, grad_query, grad_key = lax.optimization_barrier((long_got, short_got, grad_query, grad_key))
    grad_input = call(
        lambda *refs: add_kernel(0, (None, None), *refs), jax.ShapeDtypeStruct((n, step), bf16), "add_last"
    )(own_got, long_got, short_got)
    return (grad_query[None], grad_key[None], grad_value[None], grad_input[None])


def solution(mesh):
    ctx, head, pipe = (mesh.shape[name] for name in ("ctx", "head", "pipe"))
    grid = Mesh(np.asarray(mesh.devices).reshape(ctx // ROW, ROW, head, pipe), ("plane", "line", "head", "pipe"))
    seq = ("plane", "line")
    tokens = P("pipe", seq, "head")
    return jax.shard_map(
        body,
        mesh=grid,
        in_specs=(tokens, tokens, tokens, tokens, P("pipe", "head", seq), P("pipe", seq), P("pipe", None, "head")),
        out_specs=(tokens, tokens, tokens, tokens),
        check_vma=False,
    )
```
